128 devices in a mesh: section: 2 (over z_lo), ex: 16 (over x, y), tp: 4 (over z_hi, core).
Axes of the slice: x: 4, y: 4, z: 4 (z_hi: 2, z_lo: 2; z = z_hi * 2 + z_lo), core: 2. Of those that a mesh axis runs over, the one named last changes fastest.
Arguments:
- activations: bfloat16 [2, 8192, 28672], P('section', 'ex', 'tp')
- out_grads: bfloat16 [2, 8192, 8192], P('section', 'ex', 'tp')
- lengths: int32 [64], P('ex'), may hold values from 16 to 128, as said below
Outputs:
- block_kernel: float32 [64, 4], P('ex')
- cross_kernel: float32 [64, 4], P('ex')
The draws below stay inside these ranges and needn't reach their ends.
Inputs may be any that keep to these rules, and one draw needn't show every extreme that they name: `lengths`: some example has all 128 tokens live and some has 16.
All inputs are finite; a program needn't handle non-finite values.
Results may differ from the reference program's by a relative error of at most 0.0003.
Values may be sent and summed in bfloat16 or wider, within the bound.
A program may use at most 64 MiB of HBM per device.

```python
import jax
import jax.numpy as jnp
from jax import lax

D = 8192
FF = 28672
LEN = 128
EX_DEV = 4
EXAMPLES = 64
LAYERS = 2
N_EX = 16


def rough_rows(key, shape):
    first, second = jax.random.split(key)
    noise = jax.random.normal(first, shape, jnp.float32)
    spread = jnp.exp(jax.random.uniform(second, shape[:-1] + (1,), jnp.float32, -1.0, 1.0))
    return noise * spread


def draw_activations(key, part):
    return rough_rows(jax.random.fold_in(key, 11), (LAYERS, EXAMPLES * LEN, FF)).astype(jnp.bfloat16)


def draw_out_grads(key, part):
    return rough_rows(jax.random.fold_in(key, 23), (LAYERS, EXAMPLES * LEN, D)).astype(jnp.bfloat16)


def draw_lengths(key, part):
    drawn = jax.random.randint(jax.random.fold_in(key, 37), (EXAMPLES,), LEN // 8, LEN + 1, jnp.int32)
    drawn = drawn.at[0].set(LEN)
    return drawn.at[1].set(LEN // 8)


def setup_inputs(seed: int = 0) -> dict:
    splits = jax.random.split(jax.random.key(seed), 4)
    return {
        "activations": draw_activations(jax.random.fold_in(splits[3], 71), 0),
        "out_grads": draw_out_grads(jax.random.fold_in(splits[3], 71), 0),
        "lengths": draw_lengths(jax.random.fold_in(splits[3], 71), 0),
    }


def weights_of(lengths):
    slots = jnp.arange(LEN, dtype=jnp.int32)
    live = slots[None, :] < lengths[:, None]
    inverse = 1.0 / jnp.sqrt(lengths.astype(jnp.float32))
    return jnp.where(live, inverse[:, None], jnp.float32(0.0)).reshape(-1)

def tile_of(own_x, own_g, own_w, far_x, far_g, far_w):
    rows = own_x.shape[1]
    member = ((jnp.arange(rows, dtype=jnp.int32) // LEN)[:, None] == jnp.arange(EX_DEV, dtype=jnp.int32)[None, :]).astype(jnp.float32)
    left = member * own_w[:, None]
    right = member * far_w[:, None]
    total = jnp.zeros((EX_DEV, EX_DEV), jnp.float32)
    for layer in range(LAYERS):
        gram_x = jnp.dot(own_x[layer], far_x[layer].T, preferred_element_type=jnp.float32) / jnp.sqrt(jnp.float32(FF))
        gram_g = jnp.dot(own_g[layer], far_g[layer].T, preferred_element_type=jnp.float32) / jnp.sqrt(jnp.float32(D))
        product = gram_x * gram_g
        inner = jnp.dot(product, right, precision=lax.Precision.HIGHEST)
        total = total + jnp.dot(left.T, inner, precision=lax.Precision.HIGHEST)
    return total

def reference(activations, out_grads, lengths):
    rows = EX_DEV * LEN
    weight = weights_of(lengths)
    offdiag = 1.0 - jnp.eye(EX_DEV, dtype=jnp.float32)

    def one_block(index):
        partner = (index + N_EX // 2) % N_EX
        start = (index * rows).astype(jnp.int32)
        other = (partner * rows).astype(jnp.int32)
        own_x = lax.dynamic_slice_in_dim(activations, start, rows, 1)
        own_g = lax.dynamic_slice_in_dim(out_grads, start, rows, 1)
        own_w = lax.dynamic_slice_in_dim(weight, start, rows, 0)
        far_x = lax.dynamic_slice_in_dim(activations, other, rows, 1)
        far_g = lax.dynamic_slice_in_dim(out_grads, other, rows, 1)
        far_w = lax.dynamic_slice_in_dim(weight, other, rows, 0)
        block = tile_of(own_x, own_g, own_w, own_x, own_g, own_w) * offdiag
        cross = tile_of(own_x, own_g, own_w, far_x, far_g, far_w)
        return (block, cross)
    blocks, crosses = lax.map(one_block, jnp.arange(N_EX, dtype=jnp.int32))
    return (blocks.reshape(EXAMPLES, EX_DEV), crosses.reshape(EXAMPLES, EX_DEV))
```

```python
import functools

import jax
import jax.numpy as jnp
from jax import lax
from jax.experimental import pallas as pl
from jax.experimental.pallas import tpu as pltpu
from jax.sharding import PartitionSpec as P

D = 8192
FF = 28672
LEN = 128
EX_DEV = 4
ROWS = EX_DEV * LEN
WIDE = 512
N_X = 7
N_G = 2
BASE = 128
STEP = 32
MESH = pl.DeviceIdType.MESH
F32 = jnp.float32
BF16 = jnp.bfloat16


def dot_nt(left, right):
    return lax.dot_general(left, right, (((1,), (1,)), ((), ())), preferred_element_type=F32)


def place():
    s = lax.axis_index("section")
    e = lax.axis_index("ex")
    t = lax.axis_index("tp")
    return s, e, t


def remote(src, dst, send, recv, device):
    return pltpu.make_async_remote_copy(
        src_ref=src, dst_ref=dst, send_sem=send, recv_sem=recv, device_id=device, device_id_type=MESH
    )


def greet(peers):
    barrier = pltpu.get_barrier_semaphore()
    for peer in peers:
        pl.semaphore_signal(barrier, inc=1, device_id=peer, device_id_type=MESH)
    return lambda: pl.semaphore_wait(barrier, len(peers))


def iota(shape, dim):
    return lax.broadcasted_iota(jnp.int32, shape, dim)


def block_tiles(rows_ref, j, out_ref):
    at = 0
    for a in range(EX_DEV - 1):
        width = (EX_DEV - 1 - a) * LEN
        out_ref[:, at : at + width] += dot_nt(
            rows_ref[j, a * LEN : (a + 1) * LEN, :], rows_ref[j, (a + 1) * LEN :, :]
        )
        at += width


def first_kernel(
    lens, x_hbm, g_hbm,
    ok_hbm, tl_hbm, gk_hbm, gs_hbm, p1_ref, blk_ref, far_len_ref, most_ref,
    xraw, graw, xs, xk, gs, gk, far, pick, xd, gd, r_core, r_z, r_back, lt, mt, lx, ly,
    ld_sem, out_sem, s_send, s_recv, d_send, d_recv, l_send, l_recv,
):
    s, e, t = place()
    x, y = e // 4, lax.rem(e, 4)
    hi = e // 8
    core, z = lax.rem(t, 2), t // 2
    partner = (s, lax.rem(e + 8, 16), t)
    core_peer = (s, e, t + 1 - 2 * core)
    z_peer = (s, e, lax.rem(t + 2, 4))
    x_peers = [(s, lax.rem(x + d, 4) * 4 + y, t) for d in (1, 2, 3)]
    y_peers = [(s, x * 4 + lax.rem(y + d, 4), t) for d in (1, 2, 3)]
    met = greet(x_peers + y_peers + [core_peer, z_peer])

    def load_x(j):
        half = jnp.where(j < N_X, 1 - hi, hi)
        at = pl.multiple_of((half * N_X + lax.rem(j, N_X)) * WIDE, WIDE)
        return pltpu.make_async_copy(x_hbm.at[:, pl.ds(at, WIDE)], xraw.at[j], ld_sem.at[j])

    def load_g(j):
        half = 1 - hi if j < N_G else hi
        at = pl.multiple_of((half * N_G + j % N_G) * WIDE, WIDE)
        return pltpu.make_async_copy(g_hbm.at[:, pl.ds(at, WIDE)], graw.at[j], ld_sem.at[2 * N_X + j])

    for j in range(N_X):
        load_x(j).start()
    for j in range(2 * N_G):
        load_g(j).start()
    for j in range(N_X, 2 * N_X):
        load_x(j).start()

    counts = [lens[j] for j in range(EX_DEV)]
    starts = [jnp.int32(0)]
    for j in range(EX_DEV):
        starts.append(starts[-1] + counts[j])
    row = iota((8, LEN), 0)
    mine = jnp.full((8, LEN), starts[EX_DEV], jnp.int32)
    for j in range(EX_DEV):
        mine = jnp.where(row == j, counts[j], mine)
    lt[...] = mine
    for b in range(EX_DEV):
        packed = iota((LEN, LEN), 0) + b * LEN
        source = jnp.full((LEN, LEN), -1, jnp.int32)
        for j in reversed(range(EX_DEV)):
            source = jnp.where(packed < starts[j + 1], packed - starts[j] + j * LEN, source)
        for c in range(EX_DEV):
            pick[b * LEN : (b + 1) * LEN, c * LEN : (c + 1) * LEN] = jnp.where(
                source == iota((LEN, LEN), 1) + c * LEN, 1.0, 0.0
            ).astype(BF16)

    met()
    for i, peer in enumerate(x_peers):
        remote(lt, lx.at[i], l_send.at[i], l_recv.at[i], peer).start()

    def send_x(c):
        return remote(xs.at[c, pl.ds(0, BASE), :], far.at[c], s_send.at[c], s_recv.at[c], partner)

    def pack_sent(c, carry):
        load_x(c).wait()
        xs[c] = jnp.dot(pick[...], xraw[c], preferred_element_type=F32).astype(BF16)

        @pl.when(c > 0)
        def _():
            send_x(c - 1).start()

        return carry

    lax.fori_loop(0, N_X, pack_sent, 0)

    xd[...] = jnp.zeros_like(xd)
    gd[...] = jnp.zeros_like(gd)
    for j in range(2 * N_G):
        load_g(j).wait()
    send_x(N_X - 1).start()

    def gram_g(j, carry):
        block_tiles(graw, j, gd)
        return carry

    lax.fori_loop(0, 2 * N_G, gram_g, 0)
    half = LEN // 2
    keep = pl.multiple_of(core * half, half)
    give = pl.multiple_of((1 - core) * half, half)
    to_core = remote(gd.at[pl.ds(give, half)], r_core, d_send.at[0], d_recv.at[0], core_peer)
    to_core.start()

    for i in range(3):
        remote(lt, lx.at[i], l_send.at[i], l_recv.at[i], x_peers[i]).wait_recv()
    mt[...] = jnp.maximum(jnp.maximum(lt[...], lx[0]), jnp.maximum(lx[1], lx[2]))
    far_len_ref[...] = lx[1]
    def pack_g(j, carry):
        gs[j] = jnp.dot(pick[...], graw[j], preferred_element_type=F32).astype(BF16)
        gk[j] = jnp.dot(pick[...], graw[N_G + j], preferred_element_type=F32).astype(BF16)
        return carry

    lax.fori_loop(0, N_G, pack_g, 0)
    for i, peer in enumerate(y_peers):
        remote(mt, ly.at[i], l_send.at[3 + i], l_recv.at[3 + i], peer).start()

    to_core.wait()
    gd[pl.ds(keep, half), :] += r_core[...]

    def pack_kept(c, carry):
        load_x(N_X + c).wait()
        xk[c] = jnp.dot(pick[...], xraw[N_X + c], preferred_element_type=F32).astype(BF16)
        return carry

    lax.fori_loop(0, N_X, pack_kept, 0)
    to_z = remote(gd.at[pl.ds(keep, half)], r_z, d_send.at[1], d_recv.at[1], z_peer)
    to_z.start()
    outs = [
        pltpu.make_async_copy(xk, ok_hbm, out_sem.at[0]),
        pltpu.make_async_copy(xs.at[:, pl.ds(BASE, ROWS - BASE), :], tl_hbm, out_sem.at[1]),
        pltpu.make_async_copy(gk, gk_hbm, out_sem.at[2]),
        pltpu.make_async_copy(gs, gs_hbm, out_sem.at[3]),
    ]
    for out in outs:
        out.start()

    def gram_x(j, carry):
        block_tiles(xraw, j, xd)
        return carry

    lax.fori_loop(0, 2 * N_X, gram_x, 0)
    for i in range(3):
        remote(mt, ly.at[i], l_send.at[3 + i], l_recv.at[3 + i], y_peers[i]).wait_recv()
    most_ref[...] = jnp.maximum(jnp.maximum(mt[...], ly[0]), jnp.maximum(ly[1], ly[2]))

    to_z.wait()
    gd[pl.ds(keep, half), :] += r_z[...]
    p1_ref[...] = jnp.zeros_like(p1_ref)
    back = remote(gd.at[pl.ds(keep, half)], r_back, d_send.at[2], d_recv.at[2], core_peer)

    def gram_far(c, carry):
        send_x(c).wait_recv()
        p1_ref[...] += dot_nt(far[c], xk[c])
        return carry

    gram_far(0, 0)
    back.start()
    back.wait()
    gd[pl.ds(give, half), :] = r_back[...]
    blk = jnp.zeros((8, LEN), F32)
    lane = iota((8, LEN), 1)
    inner_row = iota((LEN, LEN), 0)
    inner_lane = iota((LEN, LEN), 1)
    scale_x = 1.0 / jnp.sqrt(jnp.full((LEN, LEN), float(FF), F32))
    scale_g = 1.0 / jnp.sqrt(jnp.full((LEN, LEN), float(D), F32))
    inverse = [1.0 / jnp.sqrt(jnp.full((8, LEN), counts[j].astype(F32), F32)) for j in range(EX_DEV)]
    at = 0
    for a in range(EX_DEV - 1):
        for b in range(a + 1, EX_DEV):
            product = (xd[:, at : at + LEN] * scale_x) * (gd[:, at : at + LEN] * scale_g)
            live = (inner_row < counts[a]) & (inner_lane < counts[b])
            product = jnp.where(live, product, 0.0)
            total = jnp.sum(jnp.sum(product, axis=0, keepdims=True), axis=1, keepdims=True)
            spot = ((row == a) & (lane == 8 + b)) | ((row == b) & (lane == 8 + a))
            blk = blk + jnp.where(spot, jnp.broadcast_to(total, (8, LEN)) * inverse[a] * inverse[b], 0.0)
            at += LEN
    blk_ref[...] = blk
    lax.fori_loop(1, N_X, gram_far, 0)

    def sent(c, carry):
        send_x(c).wait_send()
        return carry

    lax.fori_loop(0, N_X, sent, 0)
    for i in range(3):
        remote(lt, lx.at[i], l_send.at[i], l_recv.at[i], x_peers[i]).wait_send()
        remote(mt, ly.at[i], l_send.at[3 + i], l_recv.at[3 + i], y_peers[i]).wait_send()
    for out in outs:
        out.wait()


def second_kernel(
    size, lens, far_len, blk_ref, p1_ref, gs_hbm, gk_hbm, ok_hbm, tl_hbm,
    block_ref, cross_ref,
    own, gb, cp, cf, gg, r1, r2, r3, farx, prod, wl, acc, tile, gather, total, last,
    ld_sem, g_send, g_recv, x_send, x_recv, r_send, r_recv, t_send, t_recv,
):
    s, e, t = place()
    hi = e // 8
    core, z = lax.rem(t, 2), t // 2
    partner = (s, lax.rem(e + 8, 16), t)
    core_peer = (s, e, t + 1 - 2 * core)
    z_peer = (s, e, lax.rem(t + 2, 4))
    me = s * 4 + t
    column = []
    for d in range(1, 8):
        other = lax.rem(me + d, 8)
        column.append((other // 4, e, lax.rem(other, 4)))
    met = greet([partner] + column)
    chunks = (size - BASE) // STEP
    loads = [
        pltpu.make_async_copy(gk_hbm, gb.at[1 - hi], ld_sem.at[0]),
        pltpu.make_async_copy(ok_hbm, own, ld_sem.at[1]),
    ]
    for load in loads:
        load.start()
    met()

    def send_g(c):
        return remote(
            gs_hbm.at[c, pl.ds(0, size), :], gb.at[1 - hi, c, pl.ds(0, size), :], g_send.at[c], g_recv.at[c], partner
        )

    def got_g(c):
        return remote(
            gs_hbm.at[c, pl.ds(0, size), :], gb.at[hi, c, pl.ds(0, size), :], g_send.at[c], g_recv.at[c], partner
        )

    def send_x(c):
        at = c * STEP if isinstance(c, int) else pl.multiple_of(c * STEP, STEP)
        return remote(tl_hbm.at[:, pl.ds(at, STEP), :], farx.at[c], x_send.at[c], x_recv.at[c], partner)

    for c in range(N_G):
        send_g(c).start()
    send_x(0).start()
    send_x(1).start()

    if size < ROWS:
        gb[hi, :, size:, :] = jnp.zeros((N_G, ROWS - size, WIDE), BF16)
        cf[size:, :] = jnp.zeros((ROWS - size, ROWS), F32)
    acc[...] = jnp.zeros_like(acc)
    begin = jnp.zeros((1, LEN), jnp.int32)
    for a in range(EX_DEV):
        count = far_len[a : a + 1, :]
        inverse = 1.0 / jnp.sqrt(count.astype(F32))
        rows = iota((size, LEN), 0)
        wl[a] = jnp.where((rows >= begin) & (rows < begin + count), inverse, 0.0)
        begin = begin + count
    for load in loads:
        load.wait()

    for c in range(N_G):
        got_g(c).wait_recv()
    half, quarter = size // 2, size // 4
    for c in range(N_G):
        part = dot_nt(gb[0, c, :size, :], gb[1, c])
        cp[...] = part if c == 0 else cp[...] + part
    keep_half = pl.multiple_of(core * half, 8)
    give_half = pl.multiple_of((1 - core) * half, 8)
    keep = pl.multiple_of(core * half + z * quarter, 8)
    give = pl.multiple_of(core * half + (1 - z) * quarter, 8)

    step = remote(cp.at[pl.ds(give_half, half)], r1, r_send.at[0], r_recv.at[0], core_peer)
    step.start()
    step.wait()
    cp[pl.ds(keep_half, half), :] += r1[...]
    to_z = remote(cp.at[pl.ds(give, quarter)], r2, r_send.at[1], r_recv.at[1], z_peer)
    to_z.start()

    def take(c):
        send_x(c).wait()
        if isinstance(c, int):
            if c + 2 < chunks:
                send_x(c + 2).start()
        else:
            @pl.when(c + 2 < chunks)
            def _():
                send_x(c + 2).start()

        def add(k, total):
            return total + dot_nt(farx[c, k], own[k])

        return lax.fori_loop(0, N_X, add, jnp.zeros((STEP, ROWS), F32))

    scale_x = 1.0 / jnp.sqrt(jnp.full((STEP, LEN), float(FF), F32))

    def weigh(part, at):
        for b in range(EX_DEV):
            lanes = slice(b * LEN, (b + 1) * LEN)
            product = (part[:, lanes] * scale_x) * gg[pl.ds(at, STEP), lanes]
            for a in range(EX_DEV):
                acc[a : a + 1, lanes] += jnp.sum(product * wl[a, pl.ds(at, STEP), :], axis=0, keepdims=True)

    prod[0:STEP, :] = take(0)
    to_z.wait()
    cp[pl.ds(keep, quarter), :] += r2[...]
    to_x = remote(cp.at[pl.ds(keep, quarter)], r3, r_send.at[2], r_recv.at[2], partner)
    to_x.start()
    prod[STEP : 2 * STEP, :] = take(1)
    prod[2 * STEP : 3 * STEP, :] = take(2)
    to_x.wait()
    cf[pl.ds(keep, quarter), :] = cp[pl.ds(keep, quarter), :] + r3[...]
    back = remote(cf.at[pl.ds(keep, quarter)], cf.at[pl.ds(keep, quarter)], r_send.at[3], r_recv.at[3], z_peer)
    back.start()
    prod[3 * STEP : 4 * STEP, :] = take(3)
    back.wait_send()
    remote(cf.at[pl.ds(keep, quarter)], cf.at[pl.ds(give, quarter)], r_send.at[3], r_recv.at[3], z_peer).wait_recv()
    back = remote(cf.at[pl.ds(keep_half, half)], cf.at[pl.ds(keep_half, half)], r_send.at[4], r_recv.at[4], core_peer)
    back.start()
    back.wait_send()
    remote(
        cf.at[pl.ds(keep_half, half)], cf.at[pl.ds(give_half, half)], r_send.at[4], r_recv.at[4], core_peer
    ).wait_recv()
    scale_g = 1.0 / jnp.sqrt(jnp.full((LEN, ROWS), float(D), F32))

    @pl.when(hi == 0)
    def _():
        for i in range(EX_DEV):
            gg[i * LEN : (i + 1) * LEN, :] = cf[i * LEN : (i + 1) * LEN, :] * scale_g

    @pl.when(hi == 1)
    def _():
        for i in range(EX_DEV):
            for j in range(EX_DEV):
                turned = jnp.transpose(cf[j * LEN : (j + 1) * LEN, i * LEN : (i + 1) * LEN])
                gg[i * LEN : (i + 1) * LEN, j * LEN : (j + 1) * LEN] = turned * scale_g[:, :LEN]

    def weigh_base(i, carry):
        at = pl.multiple_of(i * STEP, STEP)
        weigh(p1_ref[pl.ds(at, STEP), :], at)
        return carry

    lax.fori_loop(0, BASE // STEP, weigh_base, 0)

    def weigh_kept(i, carry):
        at = pl.multiple_of(i * STEP, STEP)
        weigh(prod[pl.ds(at, STEP), :], pl.multiple_of(BASE + i * STEP, STEP))
        return carry

    lax.fori_loop(0, 4, weigh_kept, 0)

    def rest(c, carry):
        weigh(take(c), pl.multiple_of(BASE + c * STEP, STEP))
        return carry

    lax.fori_loop(4, chunks, rest, 0)

    lane = iota((8, LEN), 1)
    wide_row, wide_lane = iota((8, ROWS), 0), iota((8, ROWS), 1)
    right = jnp.zeros((8, ROWS), F32)
    begin = jnp.int32(0)
    for b in range(EX_DEV):
        count = lens[b]
        inverse = 1.0 / jnp.sqrt(jnp.full((8, ROWS), count.astype(F32), F32))
        inside = (wide_row == b) & (wide_lane >= begin) & (wide_lane < begin + count)
        right = jnp.where(inside, inverse, right)
        begin = begin + count
    found = acc[...]
    out = blk_ref[...]
    for a in range(EX_DEV):
        summed = jnp.sum(right * found[a : a + 1, :], axis=1, keepdims=True)
        out = out + jnp.where(lane == a, summed, 0.0)
        summed = jnp.sum(found * right[a : a + 1, :], axis=1, keepdims=True)
        out = out + jnp.where(lane == 4 + a, summed, 0.0)
    tile[...] = out
    sends = [
        remote(tile, gather.at[me], t_send.at[i], t_recv.at[me], peer) for i, peer in enumerate(column)
    ]
    for send in sends:
        send.start()
    gather[me] = out
    for d in range(1, 8):
        other = lax.rem(me + d, 8)
        remote(tile, gather.at[other], t_send.at[d - 1], t_recv.at[other], column[d - 1]).wait_recv()
    whole = gather[0]
    for i in range(1, 8):
        whole = whole + gather[i]
    total[...] = whole
    final = remote(total, last, t_send.at[7], t_recv.at[8], partner)
    final.start()
    block_ref[...] = whole[:4, 8:12]
    final.wait()
    cross_ref[...] = whole[:4, 0:4] + last[:4, 4:8]
    for send in sends:
        send.wait_send()
    for c in range(N_G):
        send_g(c).wait_send()


def vmem():
    return pl.BlockSpec(memory_space=pltpu.VMEM)


def hbm():
    return pl.BlockSpec(memory_space=pl.ANY)


def smem():
    return pl.BlockSpec(memory_space=pltpu.SMEM)


def run_first(lengths, feats, grads):
    dma = pltpu.SemaphoreType.DMA
    return pl.pallas_call(
        first_kernel,
        name="block_part",
        out_shape=(
            jax.ShapeDtypeStruct((N_X, ROWS, WIDE), BF16),
            jax.ShapeDtypeStruct((N_X, ROWS - BASE, WIDE), BF16),
            jax.ShapeDtypeStruct((N_G, ROWS, WIDE), BF16),
            jax.ShapeDtypeStruct((N_G, ROWS, WIDE), BF16),
            jax.ShapeDtypeStruct((BASE, ROWS), F32),
            jax.ShapeDtypeStruct((8, LEN), F32),
            jax.ShapeDtypeStruct((8, LEN), jnp.int32),
            jax.ShapeDtypeStruct((8, LEN), jnp.int32),
        ),
        in_specs=[smem(), hbm(), hbm()],
        out_specs=(hbm(), hbm(), hbm(), hbm(), vmem(), vmem(), vmem(), vmem()),
        scratch_shapes=[
            pltpu.VMEM((2 * N_X, ROWS, WIDE), BF16),
            pltpu.VMEM((2 * N_G, ROWS, WIDE), BF16),
            pltpu.VMEM((N_X, ROWS, WIDE), BF16),
            pltpu.VMEM((N_X, ROWS, WIDE), BF16),
            pltpu.VMEM((N_G, ROWS, WIDE), BF16),
            pltpu.VMEM((N_G, ROWS, WIDE), BF16),
            pltpu.VMEM((N_X, BASE, WIDE), BF16),
            pltpu.VMEM((ROWS, ROWS), BF16),
            pltpu.VMEM((LEN, 6 * LEN), F32),
            pltpu.VMEM((LEN, 6 * LEN), F32),
            pltpu.VMEM((LEN // 2, 6 * LEN), F32),
            pltpu.VMEM((LEN // 2, 6 * LEN), F32),
            pltpu.VMEM((LEN // 2, 6 * LEN), F32),
            pltpu.VMEM((8, LEN), jnp.int32),
            pltpu.VMEM((8, LEN), jnp.int32),
            pltpu.VMEM((3, 8, LEN), jnp.int32),
            pltpu.VMEM((3, 8, LEN), jnp.int32),
            dma((2 * N_X + 2 * N_G,)),
            dma((4,)),
            dma((N_X,)),
            dma((N_X,)),
            dma((3,)),
            dma((3,)),
            dma((6,)),
            dma((6,)),
        ],
        compiler_params=pltpu.CompilerParams(collective_id=0, has_side_effects=True, vmem_limit_bytes=56 << 20),
    )(lengths, feats, grads)


def run_second(size, lengths, far_len, blk, p1, gs, gk, ok, tl):
    dma = pltpu.SemaphoreType.DMA
    chunks = (size - BASE) // STEP
    return pl.pallas_call(
        functools.partial(second_kernel, size),
        name="cross_part_%d" % size,
        out_shape=(jax.ShapeDtypeStruct((4, 4), F32), jax.ShapeDtypeStruct((4, 4), F32)),
        in_specs=[smem(), vmem(), vmem(), vmem(), hbm(), hbm(), hbm(), hbm()],
        out_specs=(vmem(), vmem()),
        scratch_shapes=[
            pltpu.VMEM((N_X, ROWS, WIDE), BF16),
            pltpu.VMEM((2, N_G, ROWS, WIDE), BF16),
            pltpu.VMEM((size, ROWS), F32),
            pltpu.VMEM((ROWS, ROWS), F32),
            pltpu.VMEM((ROWS, ROWS), F32),
            pltpu.VMEM((size // 2, ROWS), F32),
            pltpu.VMEM((size // 4, ROWS), F32),
            pltpu.VMEM((size // 4, ROWS), F32),
            pltpu.VMEM((chunks, N_X, STEP, WIDE), BF16),
            pltpu.VMEM((4 * STEP, ROWS), F32),
            pltpu.VMEM((EX_DEV, size, LEN), F32),
            pltpu.VMEM((8, ROWS), F32),
            pltpu.VMEM((8, LEN), F32),
            pltpu.VMEM((8, 8, LEN), F32),
            pltpu.VMEM((8, LEN), F32),
            pltpu.VMEM((8, LEN), F32),
            dma((2,)),
            dma((N_G,)),
            dma((N_G,)),
            dma((chunks,)),
            dma((chunks,)),
            dma((5,)),
            dma((5,)),
            dma((8,)),
            dma((9,)),
        ],
        compiler_params=pltpu.CompilerParams(
            collective_id=size // STEP, has_side_effects=True, vmem_limit_bytes=56 << 20
        ),
    )(lengths, far_len, blk, p1, gs, gk, ok, tl)


SIZES = (512,)


def on_device(activations, out_grads, lengths):
    ok, tl, gk, gs, p1, blk, far_len, most = run_first(lengths, activations[0], out_grads[0])
    needed = most[4, 0]
    branches = [functools.partial(run_second, size) for size in SIZES]
    args = (lengths, far_len, blk, p1, gs, gk, ok, tl)
    if len(branches) == 1:
        return branches[0](*args)
    which = sum((needed > size).astype(jnp.int32) for size in SIZES[:-1])
    return lax.switch(which, branches, *args)


def solution(mesh):
    placed = (P("section", "ex", "tp"), P("section", "ex", "tp"), P("ex"))
    return jax.shard_map(
        on_device,
        mesh=mesh,
        in_specs=placed,
        out_specs=(P("ex", None), P("ex", None)),
        check_vma=False,
    )
```

```python
import functools

import jax
import jax.numpy as jnp
from jax import lax
from jax.experimental import pallas as pl
from jax.experimental.pallas import tpu as pltpu
from jax.sharding import PartitionSpec as P

D = 8192
FF = 28672
LEN = 128
EX_DEV = 4
ROWS = EX_DEV * LEN
WIDE = 512
PANEL = 256
F_TP = 14
D_TP = 4
N_X = 14
N_G = 4
TURN = 288
EVENTS = (2, 6, 8)
SURE = 16
BASE = EX_DEV * SURE
DEPTH = 2
STEP = 32
SIZES = tuple(range(288, ROWS + 1, STEP))
MESH = pl.DeviceIdType.MESH
F32 = jnp.float32
BF16 = jnp.bfloat16


def dot_nt(left, right):
    return lax.dot_general(left, right, (((1,), (1,)), ((), ())), preferred_element_type=F32)


def place():
    s = lax.axis_index("section")
    e = lax.axis_index("ex")
    t = lax.axis_index("tp")
    return s, e, t


def remote(src, dst, send, recv, device):
    return pltpu.make_async_remote_copy(
        src_ref=src, dst_ref=dst, send_sem=send, recv_sem=recv, device_id=device, device_id_type=MESH
    )


def greet(peers):
    barrier = pltpu.get_barrier_semaphore()
    for peer in peers:
        pl.semaphore_signal(barrier, inc=1, device_id=peer, device_id_type=MESH)
    return lambda: pl.semaphore_wait(barrier, len(peers))


def iota(shape, dim):
    return lax.broadcasted_iota(jnp.int32, shape, dim)


def block_tiles(rows_ref, j, out_ref):
    at = 0
    for a in range(EX_DEV - 1):
        width = (EX_DEV - 1 - a) * LEN
        out_ref[:, at : at + width] += dot_nt(
            rows_ref[j, a * LEN : (a + 1) * LEN, :], rows_ref[j, (a + 1) * LEN :, :]
        )
        at += width


def first_kernel(
    lens, x_hbm, g_hbm,
    near_hbm, pick_ref, blk_ref, far_len_ref, which_ref,
    xraw, graw, near, xd, gd, r_core, r_z, r_back, lt, mt, lx, ly,
    ld_sem, out_sem, s_send, s_recv, d_send, d_recv, l_send, l_recv,
):
    s, e, t = place()
    x, y = e // 4, lax.rem(e, 4)
    hi = e // 8
    core, z = lax.rem(t, 2), t // 2
    partner = (s, lax.rem(e + 8, 16), t)
    core_peer = (s, e, t + 1 - 2 * core)
    z_peer = (s, e, lax.rem(t + 2, 4))
    x_peers = [(s, lax.rem(x + d, 4) * 4 + y, t) for d in (1, 2, 3)]
    y_peers = [(s, x * 4 + lax.rem(y + d, 4), t) for d in (1, 2, 3)]
    met = greet(x_peers + y_peers + [core_peer, z_peer])

    def load(ref, to, j, at):
        return pltpu.make_async_copy(ref.at[:, pl.ds(pl.multiple_of(j * WIDE, WIDE), WIDE)], to.at[j], ld_sem.at[at + j])

    for j in range(D_TP):
        load(g_hbm, graw, j, 0).start()
    for j in range(F_TP):
        load(x_hbm, xraw, j, D_TP).start()

    counts = [lens[j] for j in range(EX_DEV)]
    starts = [jnp.int32(BASE)]
    for j in range(EX_DEV):
        starts.append(starts[-1] + counts[j] - SURE)
    row = iota((8, LEN), 0)
    mine = jnp.full((8, LEN), starts[EX_DEV], jnp.int32)
    for j in range(EX_DEV):
        mine = jnp.where(row == j, counts[j], mine)
    lt[...] = mine
    met()
    for i, peer in enumerate(x_peers):
        remote(lt, lx.at[i], l_send.at[i], l_recv.at[i], peer).start()

    def send_x(j):
        rows = pl.ds(j * SURE, SURE)
        at = pl.multiple_of((1 - hi) * N_X * PANEL, PANEL)
        return remote(
            x_hbm.at[pl.ds(j * LEN, SURE), pl.ds(at, N_X * PANEL)], near.at[rows], s_send.at[j], s_recv.at[j], partner
        )

    for j in range(EX_DEV):
        send_x(j).start()
    xd[...] = jnp.zeros_like(xd)
    gd[...] = jnp.zeros_like(gd)

    def gram_g(j, carry):
        load(g_hbm, graw, j, 0).wait()
        block_tiles(graw, j, gd)
        return carry

    lax.fori_loop(0, D_TP, gram_g, 0)
    half = LEN // 2
    keep = pl.multiple_of(core * half, half)
    give = pl.multiple_of((1 - core) * half, half)
    to_core = remote(gd.at[pl.ds(give, half)], r_core, d_send.at[0], d_recv.at[0], core_peer)
    to_core.start()
    for b in range(EX_DEV):
        packed = iota((LEN, LEN), 0) + b * LEN
        source = jnp.full((LEN, LEN), -1, jnp.int32)
        for j in reversed(range(EX_DEV)):
            source = jnp.where(packed < starts[j + 1], packed - starts[j] + j * LEN + SURE, source)
        if b * LEN < BASE:
            source = jnp.where(packed < BASE, packed // SURE * LEN + lax.rem(packed, SURE), source)
        for c in range(EX_DEV):
            pick_ref[b * LEN : (b + 1) * LEN, c * LEN : (c + 1) * LEN] = jnp.where(
                source == iota((LEN, LEN), 1) + c * LEN, 1.0, 0.0
            ).astype(BF16)
    to_core.wait()
    gd[pl.ds(keep, half), :] += r_core[...]
    for i in range(3):
        remote(lt, lx.at[i], l_send.at[i], l_recv.at[i], x_peers[i]).wait_recv()
    mt[...] = jnp.maximum(jnp.maximum(lt[...], lx[0]), jnp.maximum(lx[1], lx[2]))
    far_len_ref[...] = lx[1]
    to_z = remote(gd.at[pl.ds(keep, half)], r_z, d_send.at[1], d_recv.at[1], z_peer)
    to_z.start()
    for i, peer in enumerate(y_peers):
        remote(mt, ly.at[i], l_send.at[3 + i], l_recv.at[3 + i], peer).start()

    def gram_x(j, carry):
        load(x_hbm, xraw, j, D_TP).wait()
        block_tiles(xraw, j, xd)
        return carry

    lax.fori_loop(0, F_TP, gram_x, 0)
    to_z.wait()
    gd[pl.ds(keep, half), :] += r_z[...]
    back = remote(gd.at[pl.ds(keep, half)], r_back, d_send.at[2], d_recv.at[2], core_peer)
    back.start()
    for i in range(3):
        remote(mt, ly.at[i], l_send.at[3 + i], l_recv.at[3 + i], y_peers[i]).wait_recv()
    most = jnp.maximum(jnp.maximum(mt[...], ly[0]), jnp.maximum(ly[1], ly[2]))
    which = jnp.zeros((8, LEN), jnp.int32)
    for size in SIZES[:-1]:
        which = which + jnp.where(most > size, 1, 0)
    which_ref[0] = jnp.max(which)
    back.wait()
    gd[pl.ds(give, half), :] = r_back[...]
    blk = jnp.zeros((8, LEN), F32)
    lane = iota((8, LEN), 1)
    inner_row = iota((LEN, LEN), 0)
    inner_lane = iota((LEN, LEN), 1)
    scale_x = 1.0 / jnp.sqrt(jnp.full((LEN, LEN), float(FF), F32))
    scale_g = 1.0 / jnp.sqrt(jnp.full((LEN, LEN), float(D), F32))
    inverse = [1.0 / jnp.sqrt(jnp.full((8, LEN), counts[j].astype(F32), F32)) for j in range(EX_DEV)]
    at = 0
    for a in range(EX_DEV - 1):
        for b in range(a + 1, EX_DEV):
            product = (xd[:, at : at + LEN] * scale_x) * (gd[:, at : at + LEN] * scale_g)
            live = (inner_row < counts[a]) & (inner_lane < counts[b])
            product = jnp.where(live, product, 0.0)
            total = jnp.sum(jnp.sum(product, axis=0, keepdims=True), axis=1, keepdims=True)
            spot = ((row == a) & (lane == 8 + b)) | ((row == b) & (lane == 8 + a))
            blk = blk + jnp.where(spot, jnp.broadcast_to(total, (8, LEN)) * inverse[a] * inverse[b], 0.0)
            at += LEN
    blk_ref[...] = blk
    for j in range(EX_DEV):
        send_x(j).wait()
    out = pltpu.make_async_copy(near, near_hbm, out_sem.at[0])
    out.start()
    for i in range(3):
        remote(lt, lx.at[i], l_send.at[i], l_recv.at[i], x_peers[i]).wait_send()
        remote(mt, ly.at[i], l_send.at[3 + i], l_recv.at[3 + i], y_peers[i]).wait_send()
    out.wait()


def second_kernel(
    size, lens, far_len_hbm, blk_hbm, pick_hbm, near_hbm, x_hbm, g_hbm,
    out_ref,
    xraw, graw, xs, xk, gs, gb, cp, cf, gg, r1, r2, r3, farx, prod, wl, acc, tile, gather, pick, far_len, blk_ref,
    in_sem, ld_sem, lx_sem, near_sem, g_send, g_recv, x_send, x_recv, r_send, r_recv, t_send, t_recv,
):
    s, e, t = place()
    hi = e // 8
    core, z = lax.rem(t, 2), t // 2
    partner = (s, lax.rem(e + 8, 16), t)
    core_peer = (s, e, t + 1 - 2 * core)
    z_peer = (s, e, lax.rem(t + 2, 4))
    me = s * 4 + t
    column = []
    for d in range(1, 8):
        other = lax.rem(me + d, 8)
        column.append((other // 4, e, lax.rem(other, 4)))
    met = greet([partner] + column)

    def load_g(j):
        half = jnp.where(j < N_G, 1 - hi, hi)
        at = pl.multiple_of((half * N_G + lax.rem(j, N_G)) * PANEL, PANEL)
        return pltpu.make_async_copy(g_hbm.at[:, pl.ds(at, PANEL)], graw.at[j], ld_sem.at[j])

    def load_x(j):
        half = jnp.where(j < N_X, 1 - hi, hi)
        at = pl.multiple_of((half * N_X + lax.rem(j, N_X)) * PANEL, PANEL)
        return pltpu.make_async_copy(x_hbm.at[:, pl.ds(at, PANEL)], xraw.at[j], lx_sem.at[j])

    def load_near(j):
        at = pl.multiple_of(j * PANEL, PANEL)
        return pltpu.make_async_copy(near_hbm.at[:, pl.ds(at, PANEL)], farx.at[j, pl.ds(0, BASE), :], near_sem.at[j])

    def each(count, fn):
        def body(j, carry):
            fn(j)
            return carry

        lax.fori_loop(0, count, body, 0)

    small = [
        pltpu.make_async_copy(pick_hbm, pick, in_sem.at[0]),
        pltpu.make_async_copy(far_len_hbm, far_len, in_sem.at[1]),
        pltpu.make_async_copy(blk_hbm, blk_ref, in_sem.at[2]),
    ]
    small[0].start()
    each(N_G, lambda j: load_g(j).start())
    for copy in small[1:]:
        copy.start()
    each(N_G, lambda j: load_g(N_G + j).start())
    each(2 * N_X, lambda j: load_x(j).start())
    each(N_X, lambda j: load_near(j).start())

    def packed(raw, to):
        top = min(size, TURN)
        to[0:top, :] = jnp.dot(pick[0:top, :], raw[...], preferred_element_type=F32).astype(BF16)
        if size > top:
            to[top:size, :] = jnp.dot(
                pick[top:size, ROWS // 2 :], raw[ROWS // 2 :, :], preferred_element_type=F32
            ).astype(BF16)

    def pack_g_sent(c):
        load_g(c).wait()
        packed(graw.at[c], gs.at[c])

    small[0].wait()
    each(N_G, pack_g_sent)
    for copy in small[1:]:
        copy.wait()
    met()

    def send_g(c):
        return remote(
            gs.at[c], gb.at[1 - hi, c, pl.ds(0, size), :], g_send.at[c], g_recv.at[c], partner
        )

    def got_g(c):
        return remote(
            gs.at[c], gb.at[hi, c, pl.ds(0, size), :], g_send.at[c], g_recv.at[c], partner
        )

    def send_x(c):
        rows = pl.ds(BASE, size - BASE)
        return remote(xs.at[c, rows, :], farx.at[c, rows, :], x_send.at[c], x_recv.at[c], partner)

    each(N_G, lambda c: send_g(c).start())

    def pack_x_sent(c):
        load_x(c).wait()
        packed(xraw.at[c], xs.at[c])

    each(DEPTH + 1, pack_x_sent)
    for c in range(DEPTH):
        send_x(c).start()

    if size < ROWS:
        gb[:, :, size:, :] = jnp.zeros((2, N_G, ROWS - size, PANEL), BF16)
        xk[:, size:, :] = jnp.zeros((N_X, ROWS - size, PANEL), BF16)
        cf[size:, :] = jnp.zeros((ROWS - size, ROWS), F32)

    def pack_g_kept(c):
        load_g(N_G + c).wait()
        packed(graw.at[N_G + c], gb.at[1 - hi, c])

    each(N_G, pack_g_kept)

    def pack_x_rest(c, carry):
        pack_x_sent(c)
        return carry

    lax.fori_loop(DEPTH + 1, N_X, pack_x_rest, 0)

    def pack_x_kept(c):
        load_x(N_X + c).wait()
        packed(xraw.at[N_X + c], xk.at[c])

    each(N_X, pack_x_kept)
    prod[...] = jnp.zeros_like(prod)
    acc[...] = jnp.zeros_like(acc)
    begin = jnp.full((1, LEN), BASE, jnp.int32)
    for a in range(EX_DEV):
        count = far_len[a : a + 1, :]
        inverse = 1.0 / jnp.sqrt(count.astype(F32))
        rows = iota((size, LEN), 0)
        end = begin + count - SURE
        sure = (rows >= a * SURE) & (rows < (a + 1) * SURE)
        wl[a] = jnp.where(sure | ((rows >= begin) & (rows < end)), inverse, 0.0)
        begin = end
    each(N_X, lambda j: load_near(j).wait())
    each(N_G, lambda c: got_g(c).wait_recv())
    half, quarter = size // 2, size // 4
    cp[...] = jnp.zeros_like(cp)

    def gram_g(c):
        cp[...] += dot_nt(gb[0, c, 0:size, :], gb[1, c])

    each(N_G, gram_g)
    keep_half = pl.multiple_of(core * half, 8)
    give_half = pl.multiple_of((1 - core) * half, 8)
    keep = pl.multiple_of(core * half + z * quarter, 8)
    give = pl.multiple_of(core * half + (1 - z) * quarter, 8)

    step = remote(cp.at[pl.ds(give_half, half)], r1, r_send.at[0], r_recv.at[0], core_peer)
    step.start()
    step.wait()
    cp[pl.ds(keep_half, half), :] += r1[...]
    to_z = remote(cp.at[pl.ds(give, quarter)], r2, r_send.at[1], r_recv.at[1], z_peer)
    to_z.start()

    def take(c):
        send_x(c).wait()

        @pl.when(c + DEPTH < N_X)
        def _():
            send_x(c + DEPTH).start()

        prod[...] += dot_nt(farx[c], xk[c])

    def take_from(first, last):
        def body(c, carry):
            take(c)
            return carry

        lax.fori_loop(first, last, body, 0)

    take_from(0, EVENTS[0])
    to_z.wait()
    cp[pl.ds(keep, quarter), :] += r2[...]
    to_x = remote(cp.at[pl.ds(keep, quarter)], r3, r_send.at[2], r_recv.at[2], partner)
    to_x.start()
    take_from(EVENTS[0], EVENTS[1])
    to_x.wait()
    cf[pl.ds(keep, quarter), :] = cp[pl.ds(keep, quarter), :] + r3[...]
    back = remote(cf.at[pl.ds(keep, quarter)], cf.at[pl.ds(keep, quarter)], r_send.at[3], r_recv.at[3], z_peer)
    back.start()
    take_from(EVENTS[1], EVENTS[2])
    back.wait_send()
    remote(cf.at[pl.ds(keep, quarter)], cf.at[pl.ds(give, quarter)], r_send.at[3], r_recv.at[3], z_peer).wait_recv()
    back = remote(cf.at[pl.ds(keep_half, half)], cf.at[pl.ds(keep_half, half)], r_send.at[4], r_recv.at[4], core_peer)
    back.start()
    back.wait_send()
    remote(
        cf.at[pl.ds(keep_half, half)], cf.at[pl.ds(give_half, half)], r_send.at[4], r_recv.at[4], core_peer
    ).wait_recv()
    scale_g = 1.0 / jnp.sqrt(jnp.full((LEN, ROWS), float(D), F32))

    @pl.when(hi == 0)
    def _():
        for i in range(EX_DEV):
            gg[i * LEN : (i + 1) * LEN, :] = cf[i * LEN : (i + 1) * LEN, :] * scale_g

    @pl.when(hi == 1)
    def _():
        for i in range(EX_DEV):
            for j in range(EX_DEV):
                turned = jnp.transpose(cf[j * LEN : (j + 1) * LEN, i * LEN : (i + 1) * LEN])
                gg[i * LEN : (i + 1) * LEN, j * LEN : (j + 1) * LEN] = turned * scale_g[:, :LEN]

    take_from(EVENTS[2], N_X)
    scale_x = 1.0 / jnp.sqrt(jnp.full((STEP, LEN), float(FF), F32))

    def weigh(i):
        rows = pl.ds(pl.multiple_of(i * STEP, STEP), STEP)
        for b in range(EX_DEV):
            lanes = slice(b * LEN, (b + 1) * LEN)
            product = (prod[rows, lanes] * scale_x) * gg[rows, lanes]
            for a in range(EX_DEV):
                acc[a : a + 1, lanes] += jnp.sum(product * wl[a, rows, :], axis=0, keepdims=True)

    each(size // STEP, weigh)
    lane = iota((8, LEN), 1)
    wide_row, wide_lane = iota((8, ROWS), 0), iota((8, ROWS), 1)
    right = jnp.zeros((8, ROWS), F32)
    begin = jnp.int32(BASE)
    for b in range(EX_DEV):
        count = lens[b]
        inverse = 1.0 / jnp.sqrt(jnp.full((8, ROWS), count.astype(F32), F32))
        end = begin + count - SURE
        sure = (wide_lane >= b * SURE) & (wide_lane < (b + 1) * SURE)
        inside = (wide_row == b) & (sure | ((wide_lane >= begin) & (wide_lane < end)))
        right = jnp.where(inside, inverse, right)
        begin = end
    found = acc[...]
    out = blk_ref[...]
    for a in range(EX_DEV):
        summed = jnp.sum(right * found[a : a + 1, :], axis=1, keepdims=True)
        out = out + jnp.where(lane == a, summed, 0.0)
        summed = jnp.sum(found * right[a : a + 1, :], axis=1, keepdims=True)
        out = out + jnp.where(lane == 4 + a, summed, 0.0)
    tile[...] = out
    mine = hi * 8 + me

    def tell(i):
        to = lax.rem(mine + i, 16)
        other = lax.rem(to, 8)
        side = to // 8
        device = (other // 4, lax.rem(e, 8) + 8 * side, lax.rem(other, 4))
        return remote(tile, gather.at[mine], t_send.at[i], t_recv.at[mine], device)

    for i in range(1, 16):
        tell(i).start()
    gather[mine] = out
    for i in range(1, 16):
        came = lax.rem(mine + i, 16)
        remote(tile, gather.at[came], t_send.at[i], t_recv.at[came], partner).wait_recv()
    whole = gather[8 * hi]
    across = gather[8 - 8 * hi]
    for i in range(1, 8):
        whole = whole + gather[8 * hi + i]
        across = across + gather[8 - 8 * hi + i]
    out_ref[:, 0:4] = whole[:4, 0:4] + across[:4, 4:8]
    out_ref[:, 4:8] = whole[:4, 8:12]
    for i in range(1, 16):
        tell(i).wait_send()
    each(N_G, lambda c: send_g(c).wait_send())


def vmem():
    return pl.BlockSpec(memory_space=pltpu.VMEM)


def hbm():
    return pl.BlockSpec(memory_space=pl.ANY)


def smem():
    return pl.BlockSpec(memory_space=pltpu.SMEM)


def run_first(lengths, feats, grads):
    dma = pltpu.SemaphoreType.DMA
    return pl.pallas_call(
        first_kernel,
        name="block_part",
        out_shape=(
            jax.ShapeDtypeStruct((BASE, N_X * PANEL), BF16),
            jax.ShapeDtypeStruct((ROWS, ROWS), BF16),
            jax.ShapeDtypeStruct((8, LEN), F32),
            jax.ShapeDtypeStruct((8, LEN), jnp.int32),
            jax.ShapeDtypeStruct((1,), jnp.int32),
        ),
        in_specs=[smem(), hbm(), hbm()],
        out_specs=(hbm(), vmem(), vmem(), vmem(), smem()),
        scratch_shapes=[
            pltpu.VMEM((F_TP, ROWS, WIDE), BF16),
            pltpu.VMEM((D_TP, ROWS, WIDE), BF16),
            pltpu.VMEM((BASE, N_X * PANEL), BF16),
            pltpu.VMEM((LEN, 6 * LEN), F32),
            pltpu.VMEM((LEN, 6 * LEN), F32),
            pltpu.VMEM((LEN // 2, 6 * LEN), F32),
            pltpu.VMEM((LEN // 2, 6 * LEN), F32),
            pltpu.VMEM((LEN // 2, 6 * LEN), F32),
            pltpu.VMEM((8, LEN), jnp.int32),
            pltpu.VMEM((8, LEN), jnp.int32),
            pltpu.VMEM((3, 8, LEN), jnp.int32),
            pltpu.VMEM((3, 8, LEN), jnp.int32),
            dma((F_TP + D_TP,)),
            dma((1,)),
            dma((EX_DEV,)),
            dma((EX_DEV,)),
            dma((3,)),
            dma((3,)),
            dma((6,)),
            dma((6,)),
        ],
        compiler_params=pltpu.CompilerParams(collective_id=0, has_side_effects=True, vmem_limit_bytes=56 << 20),
    )(lengths, feats, grads)


def run_second(size, lengths, far_len, blk, pick, near, feats, grads):
    dma = pltpu.SemaphoreType.DMA
    return pl.pallas_call(
        functools.partial(second_kernel, size),
        name="cross_part_%d" % size,
        out_shape=jax.ShapeDtypeStruct((4, 8), F32),
        in_specs=[smem()] + [hbm()] * 6,
        out_specs=vmem(),
        scratch_shapes=[
            pltpu.VMEM((2 * N_X, ROWS, PANEL), BF16),
            pltpu.VMEM((2 * N_G, ROWS, PANEL), BF16),
            pltpu.VMEM((N_X, size, PANEL), BF16),
            pltpu.VMEM((N_X, ROWS, PANEL), BF16),
            pltpu.VMEM((N_G, size, PANEL), BF16),
            pltpu.VMEM((2, N_G, ROWS, PANEL), BF16),
            pltpu.VMEM((size, ROWS), F32),
            pltpu.VMEM((ROWS, ROWS), F32),
            pltpu.VMEM((ROWS, ROWS), F32),
            pltpu.VMEM((size // 2, ROWS), F32),
            pltpu.VMEM((size // 4, ROWS), F32),
            pltpu.VMEM((size // 4, ROWS), F32),
            pltpu.VMEM((N_X, size, PANEL), BF16),
            pltpu.VMEM((size, ROWS), F32),
            pltpu.VMEM((EX_DEV, size, LEN), F32),
            pltpu.VMEM((8, ROWS), F32),
            pltpu.VMEM((8, LEN), F32),
            pltpu.VMEM((16, 8, LEN), F32),
            pltpu.VMEM((ROWS, ROWS), BF16),
            pltpu.VMEM((8, LEN), jnp.int32),
            pltpu.VMEM((8, LEN), F32),
            dma((3,)),
            dma((2 * N_G,)),
            dma((2 * N_X,)),
            dma((N_X,)),
            dma((N_G,)),
            dma((N_G,)),
            dma((N_X,)),
            dma((N_X,)),
            dma((5,)),
            dma((5,)),
            dma((16,)),
            dma((16,)),
        ],
        compiler_params=pltpu.CompilerParams(
            collective_id=size // STEP, has_side_effects=True, vmem_limit_bytes=56 << 20
        ),
    )(lengths, far_len, blk, pick, near, feats, grads)


def on_device(activations, out_grads, lengths):
    feats, grads = activations[0], out_grads[0]
    near, pick, blk, far_len, which = run_first(lengths, feats, grads)
    branches = [functools.partial(run_second, size) for size in SIZES]
    out = lax.switch(which[0], branches, lengths, far_len, blk, pick, near, feats, grads)
    return out[:, 4:8], out[:, 0:4]


def solution(mesh):
    placed = (P("section", "ex", "tp"), P("section", "ex", "tp"), P("ex"))
    return jax.shard_map(
        on_device,
        mesh=mesh,
        in_specs=placed,
        out_specs=(P("ex", None), P("ex", None)),
        check_vma=False,
    )
```

```python
import functools

import jax
import jax.numpy as jnp
from jax import lax
from jax.experimental import pallas as pl
from jax.experimental.pallas import tpu as pltpu
from jax.sharding import PartitionSpec as P

D = 8192
FF = 28672
LEN = 128
EX_DEV = 4
ROWS = EX_DEV * LEN
WIDE = 512
PANEL = 256
NARROW = 128
F_TP = 14
D_TP = 4
X_PANELS = 28
G_PANELS = 16
SURE = 16
BASE = EX_DEV * SURE
SURE_PANELS = 10
CHUNKS = 14
G_CHUNKS = 2
DEPTH = 3
TURN = 288
EVENTS = (1, 6, 9)
VARIANTS = (
    (400, 304),
    (416, 320),
    (400, 352),
    (448, 336),
    (464, 352),
    (448, 384),
    (480, 416),
    (512, 512),
)
MESH = pl.DeviceIdType.MESH
F32 = jnp.float32
BF16 = jnp.bfloat16


def dot_nt(left, right):
    return lax.dot_general(left, right, (((1,), (1,)), ((), ())), preferred_element_type=F32)


def place():
    s = lax.axis_index("section")
    e = lax.axis_index("ex")
    t = lax.axis_index("tp")
    return s, e, t


def remote(src, dst, send, recv, device):
    return pltpu.make_async_remote_copy(
        src_ref=src, dst_ref=dst, send_sem=send, recv_sem=recv, device_id=device, device_id_type=MESH
    )


def greet(peers):
    barrier = pltpu.get_barrier_semaphore()
    for peer in peers:
        pl.semaphore_signal(barrier, inc=1, device_id=peer, device_id_type=MESH)
    return lambda: pl.semaphore_wait(barrier, len(peers))


def iota(shape, dim):
    return lax.broadcasted_iota(jnp.int32, shape, dim)


def block_tiles(rows_ref, j, out_ref):
    at = 0
    for a in range(EX_DEV - 1):
        width = (EX_DEV - 1 - a) * LEN
        out_ref[:, at : at + width] += dot_nt(
            rows_ref[j, a * LEN : (a + 1) * LEN, :], rows_ref[j, (a + 1) * LEN :, :]
        )
        at += width


def first_kernel(
    lens, x_hbm, g_hbm,
    near_hbm, pick_ref, blk_ref, far_len_ref, which_ref,
    xraw, graw, near, xd, gd, r_core, r_z, r_back, lt, mt, lx, ly,
    ld_sem, out_sem, s_send, s_recv, d_send, d_recv, l_send, l_recv,
):
    s, e, t = place()
    x, y = e // 4, lax.rem(e, 4)
    hi = e // 8
    core, z = lax.rem(t, 2), t // 2
    partner = (s, lax.rem(e + 8, 16), t)
    core_peer = (s, e, t + 1 - 2 * core)
    z_peer = (s, e, lax.rem(t + 2, 4))
    x_peers = [(s, lax.rem(x + d, 4) * 4 + y, t) for d in (1, 2, 3)]
    y_peers = [(s, x * 4 + lax.rem(y + d, 4), t) for d in (1, 2, 3)]
    met = greet(x_peers + y_peers + [core_peer, z_peer])

    def load(ref, to, j, at):
        return pltpu.make_async_copy(ref.at[:, pl.ds(pl.multiple_of(j * WIDE, WIDE), WIDE)], to.at[j], ld_sem.at[at + j])

    for j in range(D_TP):
        load(g_hbm, graw, j, 0).start()
    for j in range(F_TP):
        load(x_hbm, xraw, j, D_TP).start()

    counts = [lens[j] for j in range(EX_DEV)]
    starts = [jnp.int32(BASE)]
    for j in range(EX_DEV):
        starts.append(starts[-1] + counts[j] - SURE)
    row = iota((8, LEN), 0)
    mine = jnp.full((8, LEN), starts[EX_DEV], jnp.int32)
    for j in range(EX_DEV):
        mine = jnp.where(row == j, counts[j], mine)
    lt[...] = mine
    met()
    for i, peer in enumerate(x_peers):
        remote(lt, lx.at[i], l_send.at[i], l_recv.at[i], peer).start()

    def send_x(j):
        rows = pl.ds(j * SURE, SURE)
        at = pl.multiple_of(hi * (X_PANELS - SURE_PANELS) * PANEL, PANEL)
        source = x_hbm.at[pl.ds(j * LEN, SURE), pl.ds(at, SURE_PANELS * PANEL)]
        return remote(source, near.at[rows], s_send.at[j], s_recv.at[j], partner)

    for j in range(EX_DEV):
        send_x(j).start()
    xd[...] = jnp.zeros_like(xd)
    gd[...] = jnp.zeros_like(gd)

    def gram_g(j, carry):
        load(g_hbm, graw, j, 0).wait()
        block_tiles(graw, j, gd)
        return carry

    lax.fori_loop(0, D_TP, gram_g, 0)
    half = LEN // 2
    keep = pl.multiple_of(core * half, half)
    give = pl.multiple_of((1 - core) * half, half)
    to_core = remote(gd.at[pl.ds(give, half)], r_core, d_send.at[0], d_recv.at[0], core_peer)
    to_core.start()
    for b in range(EX_DEV):
        packed = iota((LEN, LEN), 0) + b * LEN
        source = jnp.full((LEN, LEN), -1, jnp.int32)
        for j in reversed(range(EX_DEV)):
            source = jnp.where(packed < starts[j + 1], packed - starts[j] + j * LEN + SURE, source)
        if b * LEN < BASE:
            source = jnp.where(packed < BASE, packed // SURE * LEN + lax.rem(packed, SURE), source)
        for c in range(EX_DEV):
            pick_ref[b * LEN : (b + 1) * LEN, c * LEN : (c + 1) * LEN] = jnp.where(
                source == iota((LEN, LEN), 1) + c * LEN, 1.0, 0.0
            ).astype(BF16)
    to_core.wait()
    gd[pl.ds(keep, half), :] += r_core[...]
    for i in range(3):
        remote(lt, lx.at[i], l_send.at[i], l_recv.at[i], x_peers[i]).wait_recv()
    smaller = jnp.maximum(jnp.minimum(lt[...], lx[1]), jnp.minimum(lx[0], lx[2]))
    larger = jnp.maximum(jnp.maximum(lt[...], lx[0]), jnp.maximum(lx[1], lx[2]))
    mt[...] = jnp.where(row == 5, smaller, larger)
    far_len_ref[...] = lx[1]
    to_z = remote(gd.at[pl.ds(keep, half)], r_z, d_send.at[1], d_recv.at[1], z_peer)
    to_z.start()
    for i, peer in enumerate(y_peers):
        remote(mt, ly.at[i], l_send.at[3 + i], l_recv.at[3 + i], peer).start()

    def gram_x(j, carry):
        load(x_hbm, xraw, j, D_TP).wait()
        block_tiles(xraw, j, xd)
        return carry

    lax.fori_loop(0, F_TP, gram_x, 0)
    to_z.wait()
    gd[pl.ds(keep, half), :] += r_z[...]
    back = remote(gd.at[pl.ds(keep, half)], r_back, d_send.at[2], d_recv.at[2], core_peer)
    back.start()
    for i in range(3):
        remote(mt, ly.at[i], l_send.at[3 + i], l_recv.at[3 + i], y_peers[i]).wait_recv()
    most = jnp.maximum(jnp.maximum(mt[...], ly[0]), jnp.maximum(ly[1], ly[2]))
    which = jnp.full((1, LEN), len(VARIANTS) - 1, jnp.int32)
    for i in reversed(range(len(VARIANTS) - 1)):
        fits = (most[4:5, :] <= VARIANTS[i][0]) & (most[5:6, :] <= VARIANTS[i][1])
        which = jnp.where(fits, i, which)
    which_ref[0] = jnp.max(which)
    back.wait()
    gd[pl.ds(give, half), :] = r_back[...]
    blk = jnp.zeros((8, LEN), F32)
    lane = iota((8, LEN), 1)
    inner_row = iota((LEN, LEN), 0)
    inner_lane = iota((LEN, LEN), 1)
    scale_x = 1.0 / jnp.sqrt(jnp.full((LEN, LEN), float(FF), F32))
    scale_g = 1.0 / jnp.sqrt(jnp.full((LEN, LEN), float(D), F32))
    inverse = [1.0 / jnp.sqrt(jnp.full((8, LEN), counts[j].astype(F32), F32)) for j in range(EX_DEV)]
    at = 0
    for a in range(EX_DEV - 1):
        for b in range(a + 1, EX_DEV):
            product = (xd[:, at : at + LEN] * scale_x) * (gd[:, at : at + LEN] * scale_g)
            live = (inner_row < counts[a]) & (inner_lane < counts[b])
            product = jnp.where(live, product, 0.0)
            total = jnp.sum(jnp.sum(product, axis=0, keepdims=True), axis=1, keepdims=True)
            spot = ((row == a) & (lane == 8 + b)) | ((row == b) & (lane == 8 + a))
            blk = blk + jnp.where(spot, jnp.broadcast_to(total, (8, LEN)) * inverse[a] * inverse[b], 0.0)
            at += LEN
    blk_ref[...] = blk
    for j in range(EX_DEV):
        send_x(j).wait()
    out = pltpu.make_async_copy(near, near_hbm, out_sem.at[0])
    out.start()
    for i in range(3):
        remote(lt, lx.at[i], l_send.at[i], l_recv.at[i], x_peers[i]).wait_send()
        remote(mt, ly.at[i], l_send.at[3 + i], l_recv.at[3 + i], y_peers[i]).wait_send()
    out.wait()


def up(value, step):
    return -(-value // step) * step


class Plan:
    def __init__(self, large, small):
        self.large, self.small = large, small
        self.grid = up(large, 32)
        c = min(range(SURE_PANELS, X_PANELS // 2 + 1), key=lambda c: max(c * large, (X_PANELS - c) * small))
        d = min(range(1, G_PANELS // 2 + 1), key=lambda d: max(d * large, (G_PANELS - d) * small))
        self.g_panels = (d, G_PANELS - d)
        self.x_panels = (c, X_PANELS - c)
        self.rows = (large, small)
        ends = [self.offset(r, n) for r, n in zip(self.rows, self.x_panels)]
        self.chunk = up(up(max(ends), 16) // 16, CHUNKS) // CHUNKS * 16
        g_ends = [r * n for r, n in zip(self.rows, self.g_panels)]
        self.g_chunk = up(max(g_ends) // 16, G_CHUNKS) // G_CHUNKS * 16

    def offset(self, rows, panel):
        return panel * rows - BASE * min(panel, SURE_PANELS)


def pieces(total, bounds_a, bounds_b):
    cuts = sorted({0, total} | {b for b in bounds_a + bounds_b if b < total})
    return list(zip(cuts, cuts[1:]))


def spot(bounds, first, at):
    panel = 0
    while panel + 1 < len(bounds) and bounds[panel + 1] <= at:
        panel += 1
    return panel, first[panel] + at - bounds[panel]


def second_kernel(
    plan, lens, far_len_hbm, blk_hbm, pick_hbm, near_hbm, x_hbm, g_hbm,
    out_ref,
    xraw, graw, xp, gp, sx, sg, fx, fg, nr, cp, cf, gg, r1, r2, r3, prod_l, prod_s, gram_l, gram_s,
    wl, acc, tile, gather, pick, far_len, blk_ref,
    in_sem, ld_sem, lx_sem, near_sem, g_send, g_recv, x_send, x_recv, r_send, r_recv, t_send, t_recv,
):
    large, small = plan.rows
    size = large
    s, e, t = place()
    hi = e // 8
    core, z = lax.rem(t, 2), t // 2
    partner = (s, lax.rem(e + 8, 16), t)
    core_peer = (s, e, t + 1 - 2 * core)
    z_peer = (s, e, lax.rem(t + 2, 4))
    me = s * 4 + t
    column = []
    for d in range(1, 8):
        other = lax.rem(me + d, 8)
        column.append((other // 4, e, lax.rem(other, 4)))
    met = greet([partner] + column)

    def load_g(j):
        at = pl.multiple_of(jnp.where(hi == 0, j, G_PANELS - 1 - j) * NARROW, NARROW)
        to = graw.at[j // 2, :, pl.ds(pl.multiple_of(lax.rem(j, 2) * NARROW, NARROW), NARROW)]
        return pltpu.make_async_copy(g_hbm.at[:, pl.ds(at, NARROW)], to, ld_sem.at[j])

    def load_x(j):
        at = pl.multiple_of(jnp.where(hi == 0, j, X_PANELS - 1 - j) * PANEL, PANEL)
        return pltpu.make_async_copy(x_hbm.at[:, pl.ds(at, PANEL)], xraw.at[j], lx_sem.at[j])

    def load_near(j):
        at = pl.multiple_of(jnp.where(hi == 0, SURE_PANELS - 1 - j, j) * PANEL, PANEL)
        return pltpu.make_async_copy(near_hbm.at[:, pl.ds(at, PANEL)], nr.at[j], near_sem.at[j])

    def each(first, last, fn):
        def body(j, carry):
            fn(j)
            return carry

        lax.fori_loop(first, last, body, 0)

    loads = [
        pltpu.make_async_copy(pick_hbm, pick, in_sem.at[0]),
        pltpu.make_async_copy(far_len_hbm, far_len, in_sem.at[1]),
        pltpu.make_async_copy(blk_hbm, blk_ref, in_sem.at[2]),
    ]
    for copy in loads:
        copy.start()
    each(0, G_PANELS, lambda j: load_g(j).start())
    each(0, X_PANELS, lambda j: load_x(j).start())
    each(0, SURE_PANELS, lambda j: load_near(j).start())

    def packed(raw, put):
        top = min(size, TURN)
        put(slice(0, top), jnp.dot(pick[0:top, :], raw[...], preferred_element_type=F32).astype(BF16))
        rest = jnp.dot(pick[top:size, ROWS // 2 :], raw[ROWS // 2 :, :], preferred_element_type=F32)
        put(slice(top, size), rest.astype(BF16))

    def pack_g(c):
        load_g(2 * c).wait()
        load_g(2 * c + 1).wait()

        def put(rows, value):
            gp[2 * c, rows, :] = value[:, :NARROW]
            gp[2 * c + 1, rows, :] = value[:, NARROW:]

        packed(graw.at[c], put)

    def pack_x(c):
        load_x(c).wait()

        def put(rows, value):
            xp[c, rows, :] = value

        packed(xraw.at[c], put)

    for copy in loads:
        copy.wait()
    own_total = lens[0] + lens[1] + lens[2] + lens[3]
    far_total = jnp.max(far_len[...])
    is_large = (own_total > far_total) | ((own_total == far_total) & (hi == 0))

    def fill(to, source, chunk, count, bounds, first):
        for a, b in pieces(chunk * count, *bounds):
            (pa, ra), (pb, rb) = spot(bounds[0], first[0], a), spot(bounds[1], first[1], a)
            if ra + b - a > large:
                pa, ra = pb, rb
            if rb + b - a > large:
                pb, rb = pa, ra
            if ra + b - a > large:
                pa, ra, pb, rb = 0, 0, 0, 0
            to[a:b, :] = lax.select_n(is_large, source[pb, rb : rb + b - a, :], source[pa, ra : ra + b - a, :])

    def send_g(c):
        rows = pl.ds(pl.multiple_of(c * plan.g_chunk, 16), plan.g_chunk)
        return remote(sg.at[rows], fg.at[rows], g_send.at[c], g_recv.at[c], partner)

    def send_x(c):
        rows = pl.ds(pl.multiple_of(c * plan.chunk, 16), plan.chunk)
        return remote(sx.at[rows], fx.at[rows], x_send.at[c], x_recv.at[c], partner)

    g_bounds = [[p * r for p in range(n + 1)] for r, n in zip(plan.rows, plan.g_panels)]
    x_bounds = [[plan.offset(r, p) for p in range(n + 1)] for r, n in zip(plan.rows, plan.x_panels)]
    x_first = [[BASE if p < SURE_PANELS else 0 for p in range(len(b))] for b in x_bounds]
    first_g = up(plan.g_panels[1], 2) // 2
    each(0, first_g, pack_g)
    fill(sg, gp, plan.g_chunk, G_CHUNKS, g_bounds, [[0] * len(b) for b in g_bounds])
    met()
    each(0, G_CHUNKS, lambda k: send_g(k).start())
    each(first_g, G_PANELS // 2, pack_g)

    def all_x(c):
        pack_x(c)

        @pl.when(c == plan.x_panels[1] - 1)
        def _():
            fill(sx, xp, plan.chunk, CHUNKS, x_bounds, x_first)
            each(0, DEPTH, lambda k: send_x(k).start())

    each(0, X_PANELS, all_x)
    if size < ROWS:

        def clear_g(p):
            gp[p, size:, :] = jnp.zeros((ROWS - size, NARROW), BF16)

        def clear_x(p):
            xp[p, size:, :] = jnp.zeros((ROWS - size, PANEL), BF16)

        each(0, G_PANELS, clear_g)
        each(0, X_PANELS, clear_x)
        cp[size:, :] = jnp.zeros((ROWS - size, ROWS), F32)
        cf[size:, :] = jnp.zeros((ROWS - size, ROWS), F32)
    acc[...] = jnp.zeros_like(acc)
    each(0, SURE_PANELS, lambda j: load_near(j).wait())
    def clear(i):
        rows = pl.ds(pl.multiple_of(i * 16, 16), 16)
        for ref in (prod_s, prod_l, gram_s, gram_l):
            ref[rows, :] = jnp.zeros((16, ROWS), F32)

    each(0, size // 16, clear)

    def near_part(p):
        prod_s[0:BASE, :] += dot_nt(nr[p], xp[X_PANELS - 1 - p])

    each(0, SURE_PANELS, near_part)
    prod_l[0:BASE, :] = prod_s[0:BASE, :]
    begin = jnp.full((1, LEN), BASE, jnp.int32)
    for a in range(EX_DEV):
        count = far_len[a : a + 1, :]
        inverse = 1.0 / jnp.sqrt(count.astype(F32))
        rows = iota((size, LEN), 0)
        end = begin + count - SURE
        sure = (rows >= a * SURE) & (rows < (a + 1) * SURE)
        wl[a] = jnp.where(sure | ((rows >= begin) & (rows < end)), inverse, 0.0)
        begin = end
    each(0, G_CHUNKS, lambda c: send_g(c).wait_recv())
    half, quarter = plan.grid // 2, plan.grid // 4
    for rows, count, to in ((small, plan.g_panels[1], gram_l), (large, plan.g_panels[0], gram_s)):

        def gram_part(p, rows=rows, to=to):
            at = pl.multiple_of(p * rows, 16)
            to[0:rows, :] += dot_nt(fg[pl.ds(at, rows), :], gp[G_PANELS - 1 - p])

        each(0, count, gram_part)

    def spans(i):
        i, j = i // EX_DEV, lax.rem(i, EX_DEV)
        return pl.ds(pl.multiple_of(i * LEN, LEN), LEN), pl.ds(pl.multiple_of(j * LEN, LEN), LEN)

    def turn(i, source, to):
        rows, lanes = spans(i)
        to[rows, lanes] = jnp.transpose(source[lanes, rows])

    @pl.when(hi == 0)
    def _():
        cp[0:size, :] = lax.select_n(is_large, gram_s[...], gram_l[...])

    @pl.when(hi == 1)
    def _():
        gg[0:size, :] = lax.select_n(is_large, gram_s[...], gram_l[...])
        if size < ROWS:
            gg[size:, :] = jnp.zeros((ROWS - size, ROWS), F32)
        each(0, EX_DEV * EX_DEV, lambda i: turn(i, gg, cp))

    keep_half = pl.multiple_of(core * half, 8)
    give_half = pl.multiple_of((1 - core) * half, 8)
    keep = pl.multiple_of(core * half + z * quarter, 8)
    give = pl.multiple_of(core * half + (1 - z) * quarter, 8)

    step = remote(cp.at[pl.ds(give_half, half)], r1, r_send.at[0], r_recv.at[0], core_peer)
    step.start()
    step.wait()
    cp[pl.ds(keep_half, half), :] += r1[...]
    to_z = remote(cp.at[pl.ds(give, quarter)], r2, r_send.at[1], r_recv.at[1], z_peer)
    to_z.start()

    to_x = remote(cp.at[pl.ds(keep, quarter)], r3, r_send.at[2], r_recv.at[2], partner)
    back_z = remote(cf.at[pl.ds(keep, quarter)], cf.at[pl.ds(keep, quarter)], r_send.at[3], r_recv.at[3], z_peer)
    came_z = remote(cf.at[pl.ds(keep, quarter)], cf.at[pl.ds(give, quarter)], r_send.at[3], r_recv.at[3], z_peer)
    back_core = remote(
        cf.at[pl.ds(keep_half, half)], cf.at[pl.ds(keep_half, half)], r_send.at[4], r_recv.at[4], core_peer
    )
    came_core = remote(
        cf.at[pl.ds(keep_half, half)], cf.at[pl.ds(give_half, half)], r_send.at[4], r_recv.at[4], core_peer
    )

    def panel_part(p, rows, to, sure):
        first = BASE if sure else 0
        at = p * rows - BASE * (p if sure else SURE_PANELS)
        far = fx[pl.ds(pl.multiple_of(at, 16), rows - first), :]
        to[first:rows, :] += dot_nt(far, xp[X_PANELS - 1 - p])

    scale_g = 1.0 / jnp.sqrt(jnp.full((LEN, LEN), float(D), F32))

    def scaled(i):
        rows, lanes = spans(i)
        gg[rows, lanes] = cf[rows, lanes] * scale_g

    def turn_scaled(i):
        rows, lanes = spans(i)
        gg[rows, lanes] = jnp.transpose(cf[lanes, rows]) * scale_g

    def take(c, carry):
        send_x(c).wait()

        @pl.when(c + DEPTH < CHUNKS)
        def _():
            send_x(c + DEPTH).start()

        @pl.when(c == EVENTS[0])
        def _():
            to_z.wait()
            cp[pl.ds(keep, quarter), :] += r2[...]
            to_x.start()

        @pl.when(c == EVENTS[1])
        def _():
            to_x.wait()
            cf[pl.ds(keep, quarter), :] = cp[pl.ds(keep, quarter), :] + r3[...]
            back_z.start()

        @pl.when(c == EVENTS[2])
        def _():
            back_z.wait_send()
            came_z.wait_recv()
            back_core.start()
            back_core.wait_send()
            came_core.wait_recv()

            @pl.when(hi == 0)
            def _():
                each(0, EX_DEV * EX_DEV, lambda i: scaled(i))

            @pl.when(hi == 1)
            def _():
                each(0, EX_DEV * EX_DEV, lambda i: turn_scaled(i))

        for rows, count, to in ((small, plan.x_panels[1], prod_l), (large, plan.x_panels[0], prod_s)):
            begin = SURE_PANELS * (rows - BASE)

            def sure_end(k):
                return jnp.minimum(k * plan.chunk // (rows - BASE), SURE_PANELS)

            def full_end(k):
                more = jnp.maximum(k * plan.chunk - begin, 0) // rows
                return SURE_PANELS + jnp.minimum(more, count - SURE_PANELS)

            each(sure_end(c), sure_end(c + 1), functools.partial(panel_part, rows=rows, to=to, sure=True))
            if count > SURE_PANELS:
                each(full_end(c), full_end(c + 1), functools.partial(panel_part, rows=rows, to=to, sure=False))
        return carry

    lax.fori_loop(0, CHUNKS, take, 0)
    step_rows = 32 if size % 32 == 0 else 16
    scale_x = 1.0 / jnp.sqrt(jnp.full((step_rows, LEN), float(FF), F32))

    def weigh(i):
        rows = pl.ds(pl.multiple_of(i * step_rows, step_rows), step_rows)
        for b in range(EX_DEV):
            lanes = slice(b * LEN, (b + 1) * LEN)
            gram = lax.select_n(is_large, prod_s[rows, lanes], prod_l[rows, lanes])
            product = (gram * scale_x) * gg[rows, lanes]
            for a in range(EX_DEV):
                acc[a : a + 1, lanes] += jnp.sum(product * wl[a, rows, :], axis=0, keepdims=True)

    each(0, size // step_rows, weigh)
    lane = iota((8, LEN), 1)
    wide_row, wide_lane = iota((8, ROWS), 0), iota((8, ROWS), 1)
    right = jnp.zeros((8, ROWS), F32)
    begin = jnp.int32(BASE)
    for b in range(EX_DEV):
        count = lens[b]
        inverse = 1.0 / jnp.sqrt(jnp.full((8, ROWS), count.astype(F32), F32))
        end = begin + count - SURE
        sure = (wide_lane >= b * SURE) & (wide_lane < (b + 1) * SURE)
        inside = (wide_row == b) & (sure | ((wide_lane >= begin) & (wide_lane < end)))
        right = jnp.where(inside, inverse, right)
        begin = end
    found = acc[...]
    out = blk_ref[...]
    for a in range(EX_DEV):
        summed = jnp.sum(right * found[a : a + 1, :], axis=1, keepdims=True)
        out = out + jnp.where(lane == a, summed, 0.0)
        summed = jnp.sum(found * right[a : a + 1, :], axis=1, keepdims=True)
        out = out + jnp.where(lane == 4 + a, summed, 0.0)
    tile[...] = out
    mine = hi * 8 + me

    def tell(i):
        to = lax.rem(mine + i, 16)
        other = lax.rem(to, 8)
        side = to // 8
        device = (other // 4, lax.rem(e, 8) + 8 * side, lax.rem(other, 4))
        return remote(tile, gather.at[mine], t_send.at[i], t_recv.at[mine], device)

    for i in range(1, 16):
        tell(i).start()
    gather[mine] = out
    for i in range(1, 16):
        came = lax.rem(mine + i, 16)
        remote(tile, gather.at[came], t_send.at[i], t_recv.at[came], partner).wait_recv()
    whole = gather[8 * hi]
    across = gather[8 - 8 * hi]
    for i in range(1, 8):
        whole = whole + gather[8 * hi + i]
        across = across + gather[8 - 8 * hi + i]
    out_ref[:, 0:4] = whole[:4, 0:4] + across[:4, 4:8]
    out_ref[:, 4:8] = whole[:4, 8:12]
    for i in range(1, 16):
        tell(i).wait_send()
    each(0, G_CHUNKS, lambda c: send_g(c).wait_send())


def vmem():
    return pl.BlockSpec(memory_space=pltpu.VMEM)


def hbm():
    return pl.BlockSpec(memory_space=pl.ANY)


def smem():
    return pl.BlockSpec(memory_space=pltpu.SMEM)


def run_first(lengths, feats, grads):
    dma = pltpu.SemaphoreType.DMA
    return pl.pallas_call(
        first_kernel,
        name="block_part",
        out_shape=(
            jax.ShapeDtypeStruct((BASE, SURE_PANELS * PANEL), BF16),
            jax.ShapeDtypeStruct((ROWS, ROWS), BF16),
            jax.ShapeDtypeStruct((8, LEN), F32),
            jax.ShapeDtypeStruct((8, LEN), jnp.int32),
            jax.ShapeDtypeStruct((1,), jnp.int32),
        ),
        in_specs=[smem(), hbm(), hbm()],
        out_specs=(hbm(), vmem(), vmem(), vmem(), smem()),
        scratch_shapes=[
            pltpu.VMEM((F_TP, ROWS, WIDE), BF16),
            pltpu.VMEM((D_TP, ROWS, WIDE), BF16),
            pltpu.VMEM((BASE, SURE_PANELS * PANEL), BF16),
            pltpu.VMEM((LEN, 6 * LEN), F32),
            pltpu.VMEM((LEN, 6 * LEN), F32),
            pltpu.VMEM((LEN // 2, 6 * LEN), F32),
            pltpu.VMEM((LEN // 2, 6 * LEN), F32),
            pltpu.VMEM((LEN // 2, 6 * LEN), F32),
            pltpu.VMEM((8, LEN), jnp.int32),
            pltpu.VMEM((8, LEN), jnp.int32),
            pltpu.VMEM((3, 8, LEN), jnp.int32),
            pltpu.VMEM((3, 8, LEN), jnp.int32),
            dma((F_TP + D_TP,)),
            dma((1,)),
            dma((EX_DEV,)),
            dma((EX_DEV,)),
            dma((3,)),
            dma((3,)),
            dma((6,)),
            dma((6,)),
        ],
        compiler_params=pltpu.CompilerParams(collective_id=0, has_side_effects=True, vmem_limit_bytes=56 << 20),
    )(lengths, feats, grads)


def run_second(number, lengths, far_len, blk, pick, near, feats, grads):
    dma = pltpu.SemaphoreType.DMA
    plan = Plan(*VARIANTS[number])
    stream, g_stream = plan.chunk * CHUNKS, plan.g_chunk * G_CHUNKS
    tall = pltpu.VMEM((plan.large, ROWS), F32)
    square = pltpu.VMEM((ROWS, ROWS), F32)
    return pl.pallas_call(
        functools.partial(second_kernel, plan),
        name="cross_part_%d_%d" % plan.rows,
        out_shape=jax.ShapeDtypeStruct((4, 8), F32),
        in_specs=[smem()] + [hbm()] * 6,
        out_specs=vmem(),
        scratch_shapes=[
            pltpu.VMEM((X_PANELS, ROWS, PANEL), BF16),
            pltpu.VMEM((G_PANELS // 2, ROWS, 2 * NARROW), BF16),
            pltpu.VMEM((X_PANELS, ROWS, PANEL), BF16),
            pltpu.VMEM((G_PANELS, ROWS, NARROW), BF16),
            pltpu.VMEM((stream, PANEL), BF16),
            pltpu.VMEM((g_stream, NARROW), BF16),
            pltpu.VMEM((stream, PANEL), BF16),
            pltpu.VMEM((g_stream, NARROW), BF16),
            pltpu.VMEM((SURE_PANELS, BASE, PANEL), BF16),
            square,
            square,
            square,
            pltpu.VMEM((plan.grid // 2, ROWS), F32),
            pltpu.VMEM((plan.grid // 4, ROWS), F32),
            pltpu.VMEM((plan.grid // 4, ROWS), F32),
            tall,
            tall,
            tall,
            tall,
            pltpu.VMEM((EX_DEV, plan.large, LEN), F32),
            pltpu.VMEM((8, ROWS), F32),
            pltpu.VMEM((8, LEN), F32),
            pltpu.VMEM((16, 8, LEN), F32),
            pltpu.VMEM((ROWS, ROWS), BF16),
            pltpu.VMEM((8, LEN), jnp.int32),
            pltpu.VMEM((8, LEN), F32),
            dma((3,)),
            dma((G_PANELS,)),
            dma((X_PANELS,)),
            dma((SURE_PANELS,)),
            dma((G_CHUNKS,)),
            dma((G_CHUNKS,)),
            dma((CHUNKS,)),
            dma((CHUNKS,)),
            dma((5,)),
            dma((5,)),
            dma((16,)),
            dma((16,)),
        ],
        compiler_params=pltpu.CompilerParams(
            collective_id=number + 1, has_side_effects=True, vmem_limit_bytes=60 << 20
        ),
    )(lengths, far_len, blk, pick, near, feats, grads)


def on_device(activations, out_grads, lengths):
    feats, grads = activations[0], out_grads[0]
    near, pick, blk, far_len, which = run_first(lengths, feats, grads)
    branches = [functools.partial(run_second, number) for number in range(len(VARIANTS))]
    out = lax.switch(which[0], branches, lengths, far_len, blk, pick, near, feats, grads)
    return out[:, 4:8], out[:, 0:4]


def solution(mesh):
    placed = (P("section", "ex", "tp"), P("section", "ex", "tp"), P("ex"))
    return jax.shard_map(
        on_device,
        mesh=mesh,
        in_specs=placed,
        out_specs=(P("ex", None), P("ex", None)),
        check_vma=False,
    )
```

```python
import functools

import jax
import jax.numpy as jnp
from jax import lax
from jax.experimental import pallas as pl
from jax.experimental.pallas import tpu as pltpu
from jax.sharding import PartitionSpec as P

D = 8192
FF = 28672
LEN = 128
EX_DEV = 4
ROWS = EX_DEV * LEN
WIDE = 512
PANEL = 256
NARROW = 128
F_TP = 14
D_TP = 4
X_PANELS = 28
G_PANELS = 16
SURE = 16
BASE = EX_DEV * SURE
SURE_PANELS = 12
G_CHUNKS = 2
DEPTH = 5
TURN = 288
VARIANTS = (
    (400, 304),
    (416, 320),
    (400, 352),
    (448, 336),
    (464, 352),
    (448, 384),
    (480, 416),
    (512, 512),
)
MESH = pl.DeviceIdType.MESH
F32 = jnp.float32
BF16 = jnp.bfloat16


def dot_nt(left, right):
    return lax.dot_general(left, right, (((1,), (1,)), ((), ())), preferred_element_type=F32)


def place():
    s = lax.axis_index("section")
    e = lax.axis_index("ex")
    t = lax.axis_index("tp")
    return s, e, t


def remote(src, dst, send, recv, device):
    return pltpu.make_async_remote_copy(
        src_ref=src, dst_ref=dst, send_sem=send, recv_sem=recv, device_id=device, device_id_type=MESH
    )


def greet(peers):
    barrier = pltpu.get_barrier_semaphore()
    for peer in peers:
        pl.semaphore_signal(barrier, inc=1, device_id=peer, device_id_type=MESH)
    return lambda: pl.semaphore_wait(barrier, len(peers))


def iota(shape, dim):
    return lax.broadcasted_iota(jnp.int32, shape, dim)


def block_tiles(rows_ref, j, out_ref):
    at = 0
    for a in range(EX_DEV - 1):
        width = (EX_DEV - 1 - a) * LEN
        out_ref[:, at : at + width] += dot_nt(
            rows_ref[j, a * LEN : (a + 1) * LEN, :], rows_ref[j, (a + 1) * LEN :, :]
        )
        at += width


def first_kernel(
    lens, x_hbm, g_hbm,
    near_hbm, pick_ref, blk_ref, far_len_ref, which_ref,
    xraw, graw, near, xd, gd, r_core, r_z, r_back, lt, mt, lx, ly,
    ld_sem, out_sem, s_send, s_recv, d_send, d_recv, l_send, l_recv,
):
    s, e, t = place()
    x, y = e // 4, lax.rem(e, 4)
    hi = e // 8
    core, z = lax.rem(t, 2), t // 2
    partner = (s, lax.rem(e + 8, 16), t)
    core_peer = (s, e, t + 1 - 2 * core)
    z_peer = (s, e, lax.rem(t + 2, 4))
    x_peers = [(s, lax.rem(x + d, 4) * 4 + y, t) for d in (1, 2, 3)]
    y_peers = [(s, x * 4 + lax.rem(y + d, 4), t) for d in (1, 2, 3)]
    met = greet(x_peers + y_peers + [core_peer, z_peer])

    def load(ref, to, j, at):
        return pltpu.make_async_copy(ref.at[:, pl.ds(pl.multiple_of(j * WIDE, WIDE), WIDE)], to.at[j], ld_sem.at[at + j])

    for j in range(D_TP):
        load(g_hbm, graw, j, 0).start()
    for j in range(F_TP):
        load(x_hbm, xraw, j, D_TP).start()

    counts = [lens[j] for j in range(EX_DEV)]
    starts = [jnp.int32(BASE)]
    for j in range(EX_DEV):
        starts.append(starts[-1] + counts[j] - SURE)
    row = iota((8, LEN), 0)
    mine = jnp.full((8, LEN), starts[EX_DEV], jnp.int32)
    for j in range(EX_DEV):
        mine = jnp.where(row == j, counts[j], mine)
    lt[...] = mine
    xd[...] = jnp.zeros_like(xd)
    gd[...] = jnp.zeros_like(gd)

    def gram_g(j, carry):
        load(g_hbm, graw, j, 0).wait()
        block_tiles(graw, j, gd)
        return carry

    lax.fori_loop(0, D_TP, gram_g, 0)
    met()
    for i, peer in enumerate(x_peers):
        remote(lt, lx.at[i], l_send.at[i], l_recv.at[i], peer).start()

    def send_x(j):
        rows = pl.ds(j * SURE, SURE)
        at = pl.multiple_of(hi * (X_PANELS - SURE_PANELS) * PANEL, PANEL)
        source = x_hbm.at[pl.ds(j * LEN, SURE), pl.ds(at, SURE_PANELS * PANEL)]
        return remote(source, near.at[rows], s_send.at[j], s_recv.at[j], partner)

    for j in range(EX_DEV):
        send_x(j).start()
    half = LEN // 2
    keep = pl.multiple_of(core * half, half)
    give = pl.multiple_of((1 - core) * half, half)
    to_core = remote(gd.at[pl.ds(give, half)], r_core, d_send.at[0], d_recv.at[0], core_peer)
    to_core.start()
    for b in range(EX_DEV):
        packed = iota((LEN, LEN), 0) + b * LEN
        source = jnp.full((LEN, LEN), -1, jnp.int32)
        for j in reversed(range(EX_DEV)):
            source = jnp.where(packed < starts[j + 1], packed - starts[j] + j * LEN + SURE, source)
        if b * LEN < BASE:
            source = jnp.where(packed < BASE, packed // SURE * LEN + lax.rem(packed, SURE), source)
        for c in range(EX_DEV):
            pick_ref[b * LEN : (b + 1) * LEN, c * LEN : (c + 1) * LEN] = jnp.where(
                source == iota((LEN, LEN), 1) + c * LEN, 1.0, 0.0
            ).astype(BF16)
    to_core.wait()
    gd[pl.ds(keep, half), :] += r_core[...]
    for i in range(3):
        remote(lt, lx.at[i], l_send.at[i], l_recv.at[i], x_peers[i]).wait_recv()
    smaller = jnp.maximum(jnp.minimum(lt[...], lx[1]), jnp.minimum(lx[0], lx[2]))
    larger = jnp.maximum(jnp.maximum(lt[...], lx[0]), jnp.maximum(lx[1], lx[2]))
    mt[...] = jnp.where(row == 5, smaller, larger)
    far_len_ref[...] = lx[1]
    to_z = remote(gd.at[pl.ds(keep, half)], r_z, d_send.at[1], d_recv.at[1], z_peer)
    to_z.start()
    for i, peer in enumerate(y_peers):
        remote(mt, ly.at[i], l_send.at[3 + i], l_recv.at[3 + i], peer).start()

    def gram_x(j, carry):
        load(x_hbm, xraw, j, D_TP).wait()
        block_tiles(xraw, j, xd)
        return carry

    lax.fori_loop(0, F_TP, gram_x, 0)
    to_z.wait()
    gd[pl.ds(keep, half), :] += r_z[...]
    back = remote(gd.at[pl.ds(keep, half)], r_back, d_send.at[2], d_recv.at[2], core_peer)
    back.start()
    for i in range(3):
        remote(mt, ly.at[i], l_send.at[3 + i], l_recv.at[3 + i], y_peers[i]).wait_recv()
    most = jnp.maximum(jnp.maximum(mt[...], ly[0]), jnp.maximum(ly[1], ly[2]))
    which = jnp.full((1, LEN), len(VARIANTS) - 1, jnp.int32)
    for i in reversed(range(len(VARIANTS) - 1)):
        fits = (most[4:5, :] <= VARIANTS[i][0]) & (most[5:6, :] <= VARIANTS[i][1])
        which = jnp.where(fits, i, which)
    which_ref[0] = jnp.max(which)
    back.wait()
    gd[pl.ds(give, half), :] = r_back[...]
    blk = jnp.zeros((8, LEN), F32)
    lane = iota((8, LEN), 1)
    inner_row = iota((LEN, LEN), 0)
    inner_lane = iota((LEN, LEN), 1)
    scale_x = 1.0 / jnp.sqrt(jnp.full((LEN, LEN), float(FF), F32))
    scale_g = 1.0 / jnp.sqrt(jnp.full((LEN, LEN), float(D), F32))
    inverse = [1.0 / jnp.sqrt(jnp.full((8, LEN), counts[j].astype(F32), F32)) for j in range(EX_DEV)]
    at = 0
    for a in range(EX_DEV - 1):
        for b in range(a + 1, EX_DEV):
            product = (xd[:, at : at + LEN] * scale_x) * (gd[:, at : at + LEN] * scale_g)
            live = (inner_row < counts[a]) & (inner_lane < counts[b])
            product = jnp.where(live, product, 0.0)
            total = jnp.sum(jnp.sum(product, axis=0, keepdims=True), axis=1, keepdims=True)
            spot = ((row == a) & (lane == 8 + b)) | ((row == b) & (lane == 8 + a))
            blk = blk + jnp.where(spot, jnp.broadcast_to(total, (8, LEN)) * inverse[a] * inverse[b], 0.0)
            at += LEN
    blk_ref[...] = blk
    for j in range(EX_DEV):
        send_x(j).wait()
    out = pltpu.make_async_copy(near, near_hbm, out_sem.at[0])
    out.start()
    for i in range(3):
        remote(lt, lx.at[i], l_send.at[i], l_recv.at[i], x_peers[i]).wait_send()
        remote(mt, ly.at[i], l_send.at[3 + i], l_recv.at[3 + i], y_peers[i]).wait_send()
    out.wait()


def up(value, step):
    return -(-value // step) * step


class Plan:
    def __init__(self, large, small):
        self.large, self.small = large, small
        self.grid = up(large, 32)
        c = min(range(SURE_PANELS, X_PANELS // 2 + 1), key=lambda c: max(c * large, (X_PANELS - c) * small))
        d = min(range(1, G_PANELS // 2 + 1), key=lambda d: max(d * large, (G_PANELS - d) * small))
        self.g_panels = (d, G_PANELS - d)
        self.x_panels = (c, X_PANELS - c)
        self.rows = (large, small)
        ends = [self.offset(r, n) for r, n in zip(self.rows, self.x_panels)]
        units = up(max(ends), 16) // 16
        self.chunks = min(range(11, 18), key=lambda n: (up(units, n), -n))
        self.chunk = up(units, self.chunks) // self.chunks * 16
        self.events = (1, self.chunks * 6 // 14, self.chunks * 9 // 14)
        g_ends = [r * n for r, n in zip(self.rows, self.g_panels)]
        self.g_chunk = up(max(g_ends) // 16, G_CHUNKS) // G_CHUNKS * 16

    def offset(self, rows, panel):
        return panel * rows - BASE * min(panel, SURE_PANELS)


def pieces(total, bounds_a, bounds_b):
    cuts = sorted({0, total} | {b for b in bounds_a + bounds_b if b < total})
    return list(zip(cuts, cuts[1:]))


def spot(bounds, first, at):
    panel = 0
    while panel + 1 < len(bounds) and bounds[panel + 1] <= at:
        panel += 1
    return panel, first[panel] + at - bounds[panel]


def second_kernel(
    plan, lens, far_len_hbm, blk_hbm, pick_hbm, near_hbm, x_hbm, g_hbm,
    out_ref,
    xraw, graw, xp, gp, sx, sg, fx, fg, nr, cp, cf, gg, r1, r2, r3, prod_l, prod_s, gram_l, gram_s,
    wl, acc, right_ref, tile, gather, pick, far_len, blk_ref,
    in_sem, ld_sem, lx_sem, near_sem, g_send, g_recv, x_send, x_recv, r_send, r_recv, t_send, t_recv,
):
    large, small = plan.rows
    size = large
    s, e, t = place()
    hi = e // 8
    core, z = lax.rem(t, 2), t // 2
    partner = (s, lax.rem(e + 8, 16), t)
    core_peer = (s, e, t + 1 - 2 * core)
    z_peer = (s, e, lax.rem(t + 2, 4))
    me = s * 4 + t
    column = []
    for d in range(1, 8):
        other = lax.rem(me + d, 8)
        column.append((other // 4, e, lax.rem(other, 4)))
    met = greet([partner] + column)

    def load_g(j):
        at = pl.multiple_of(jnp.where(hi == 0, j, G_PANELS - 1 - j) * NARROW, NARROW)
        to = graw.at[j // 2, :, pl.ds(pl.multiple_of(lax.rem(j, 2) * NARROW, NARROW), NARROW)]
        return pltpu.make_async_copy(g_hbm.at[:, pl.ds(at, NARROW)], to, ld_sem.at[j])

    def load_x(j):
        at = pl.multiple_of(jnp.where(hi == 0, j, X_PANELS - 1 - j) * PANEL, PANEL)
        return pltpu.make_async_copy(x_hbm.at[:, pl.ds(at, PANEL)], xraw.at[j], lx_sem.at[j])

    def load_near(j):
        at = pl.multiple_of(jnp.where(hi == 0, SURE_PANELS - 1 - j, j) * PANEL, PANEL)
        return pltpu.make_async_copy(near_hbm.at[:, pl.ds(at, PANEL)], nr.at[j], near_sem.at[j])

    def each(first, last, fn):
        def body(j, carry):
            fn(j)
            return carry

        lax.fori_loop(first, last, body, 0)

    loads = [
        pltpu.make_async_copy(pick_hbm, pick, in_sem.at[0]),
        pltpu.make_async_copy(far_len_hbm, far_len, in_sem.at[1]),
        pltpu.make_async_copy(blk_hbm, blk_ref, in_sem.at[2]),
    ]
    for copy in loads:
        copy.start()
    each(0, G_PANELS, lambda j: load_g(j).start())
    each(0, X_PANELS, lambda j: load_x(j).start())
    each(0, SURE_PANELS, lambda j: load_near(j).start())

    def packed(raw, put):
        top = min(size, TURN)
        put(slice(0, top), jnp.dot(pick[0:top, :], raw[...], preferred_element_type=F32).astype(BF16))
        rest = jnp.dot(pick[top:size, ROWS // 2 :], raw[ROWS // 2 :, :], preferred_element_type=F32)
        put(slice(top, size), rest.astype(BF16))

    def pack_g(c):
        load_g(2 * c).wait()
        load_g(2 * c + 1).wait()

        def put(rows, value):
            gp[2 * c, rows, :] = value[:, :NARROW]
            gp[2 * c + 1, rows, :] = value[:, NARROW:]

        packed(graw.at[c], put)

    def pack_x(c):
        load_x(c).wait()

        def put(rows, value):
            xp[c, rows, :] = value

        packed(xraw.at[c], put)

    for copy in loads:
        copy.wait()
    own_total = lens[0] + lens[1] + lens[2] + lens[3]
    far_total = jnp.max(far_len[...])
    is_large = (own_total > far_total) | ((own_total == far_total) & (hi == 0))

    def fill(to, source, chunk, count, bounds, first):
        for a, b in pieces(chunk * count, *bounds):
            (pa, ra), (pb, rb) = spot(bounds[0], first[0], a), spot(bounds[1], first[1], a)
            if ra + b - a > large:
                pa, ra = pb, rb
            if rb + b - a > large:
                pb, rb = pa, ra
            if ra + b - a > large:
                pa, ra, pb, rb = 0, 0, 0, 0
            to[a:b, :] = lax.select_n(is_large, source[pb, rb : rb + b - a, :], source[pa, ra : ra + b - a, :])

    def send_g(c):
        rows = pl.ds(pl.multiple_of(c * plan.g_chunk, 16), plan.g_chunk)
        return remote(sg.at[rows], fg.at[rows], g_send.at[c], g_recv.at[c], partner)

    def send_x(c):
        rows = pl.ds(pl.multiple_of(c * plan.chunk, 16), plan.chunk)
        return remote(sx.at[rows], fx.at[rows], x_send.at[c], x_recv.at[c], partner)

    g_bounds = [[p * r for p in range(n + 1)] for r, n in zip(plan.rows, plan.g_panels)]
    x_bounds = [[plan.offset(r, p) for p in range(n + 1)] for r, n in zip(plan.rows, plan.x_panels)]
    x_first = [[BASE if p < SURE_PANELS else 0 for p in range(len(b))] for b in x_bounds]
    first_g = up(plan.g_panels[1], 2) // 2
    each(0, first_g, pack_g)
    fill(sg, gp, plan.g_chunk, G_CHUNKS, g_bounds, [[0] * len(b) for b in g_bounds])
    met()
    each(0, G_CHUNKS, lambda k: send_g(k).start())
    each(first_g, G_PANELS // 2, pack_g)

    def all_x(c):
        pack_x(c)

        @pl.when(c == plan.x_panels[1] - 1)
        def _():
            fill(sx, xp, plan.chunk, plan.chunks, x_bounds, x_first)
            each(0, DEPTH, lambda k: send_x(k).start())

    each(0, X_PANELS, all_x)
    if size < ROWS:

        def clear_g(p):
            gp[p, size:, :] = jnp.zeros((ROWS - size, NARROW), BF16)

        def clear_x(p):
            xp[p, size:, :] = jnp.zeros((ROWS - size, PANEL), BF16)

        each(0, G_PANELS, clear_g)
        each(0, X_PANELS, clear_x)
        cp[size:, :] = jnp.zeros((ROWS - size, ROWS), F32)
        cf[size:, :] = jnp.zeros((ROWS - size, ROWS), F32)
    acc[...] = jnp.zeros_like(acc)
    wide_row, wide_lane = iota((8, ROWS), 0), iota((8, ROWS), 1)
    right = jnp.zeros((8, ROWS), F32)
    begin = jnp.int32(BASE)
    for b in range(EX_DEV):
        count = lens[b]
        inverse = 1.0 / jnp.sqrt(jnp.full((8, ROWS), count.astype(F32), F32))
        end = begin + count - SURE
        sure = (wide_lane >= b * SURE) & (wide_lane < (b + 1) * SURE)
        inside = (wide_row == b) & (sure | ((wide_lane >= begin) & (wide_lane < end)))
        right = jnp.where(inside, inverse, right)
        begin = end
    right_ref[...] = right
    each(0, SURE_PANELS, lambda j: load_near(j).wait())
    def clear(i):
        rows = pl.ds(pl.multiple_of(i * 16, 16), 16)
        for ref in (prod_s, prod_l, gram_s, gram_l):
            ref[rows, :] = jnp.zeros((16, ROWS), F32)

    each(0, size // 16, clear)

    def near_part(p):
        prod_s[0:BASE, :] += dot_nt(nr[p], xp[X_PANELS - 1 - p])

    each(0, SURE_PANELS, near_part)
    prod_l[0:BASE, :] = prod_s[0:BASE, :]
    begin = jnp.full((1, LEN), BASE, jnp.int32)
    for a in range(EX_DEV):
        count = far_len[a : a + 1, :]
        inverse = 1.0 / jnp.sqrt(count.astype(F32))
        rows = iota((size, LEN), 0)
        end = begin + count - SURE
        sure = (rows >= a * SURE) & (rows < (a + 1) * SURE)
        wl[a] = jnp.where(sure | ((rows >= begin) & (rows < end)), inverse, 0.0)
        begin = end
    each(0, G_CHUNKS, lambda c: send_g(c).wait_recv())
    half, quarter = plan.grid // 2, plan.grid // 4
    for rows, count, to in ((small, plan.g_panels[1], gram_l), (large, plan.g_panels[0], gram_s)):

        def gram_part(p, rows=rows, to=to):
            at = pl.multiple_of(p * rows, 16)
            to[0:rows, :] += dot_nt(fg[pl.ds(at, rows), :], gp[G_PANELS - 1 - p])

        each(0, count, gram_part)

    def spans(i):
        i, j = i // EX_DEV, lax.rem(i, EX_DEV)
        return pl.ds(pl.multiple_of(i * LEN, LEN), LEN), pl.ds(pl.multiple_of(j * LEN, LEN), LEN)

    def turn(i, source, to):
        rows, lanes = spans(i)
        to[rows, lanes] = jnp.transpose(source[lanes, rows])

    @pl.when(hi == 0)
    def _():
        cp[0:size, :] = lax.select_n(is_large, gram_s[...], gram_l[...])

    @pl.when(hi == 1)
    def _():
        gg[0:size, :] = lax.select_n(is_large, gram_s[...], gram_l[...])
        if size < ROWS:
            gg[size:, :] = jnp.zeros((ROWS - size, ROWS), F32)
        each(0, EX_DEV * EX_DEV, lambda i: turn(i, gg, cp))

    keep_half = pl.multiple_of(core * half, 8)
    give_half = pl.multiple_of((1 - core) * half, 8)
    keep = pl.multiple_of(core * half + z * quarter, 8)
    give = pl.multiple_of(core * half + (1 - z) * quarter, 8)

    step = remote(cp.at[pl.ds(give_half, half)], r1, r_send.at[0], r_recv.at[0], core_peer)
    step.start()
    step.wait()
    cp[pl.ds(keep_half, half), :] += r1[...]
    to_z = remote(cp.at[pl.ds(give, quarter)], r2, r_send.at[1], r_recv.at[1], z_peer)
    to_z.start()

    to_x = remote(cp.at[pl.ds(keep, quarter)], r3, r_send.at[2], r_recv.at[2], partner)
    back_z = remote(cf.at[pl.ds(keep, quarter)], cf.at[pl.ds(keep, quarter)], r_send.at[3], r_recv.at[3], z_peer)
    came_z = remote(cf.at[pl.ds(keep, quarter)], cf.at[pl.ds(give, quarter)], r_send.at[3], r_recv.at[3], z_peer)
    back_core = remote(
        cf.at[pl.ds(keep_half, half)], cf.at[pl.ds(keep_half, half)], r_send.at[4], r_recv.at[4], core_peer
    )
    came_core = remote(
        cf.at[pl.ds(keep_half, half)], cf.at[pl.ds(give_half, half)], r_send.at[4], r_recv.at[4], core_peer
    )

    def panel_part(p, rows, to, sure):
        first = BASE if sure else 0
        at = p * rows - BASE * (p if sure else SURE_PANELS)
        far = fx[pl.ds(pl.multiple_of(at, 16), rows - first), :]
        to[first:rows, :] += dot_nt(far, xp[X_PANELS - 1 - p])

    scale_g = 1.0 / jnp.sqrt(jnp.full((LEN, LEN), float(D), F32))

    def scaled(i):
        rows, lanes = spans(i)
        gg[rows, lanes] = cf[rows, lanes] * scale_g

    def turn_scaled(i):
        rows, lanes = spans(i)
        gg[rows, lanes] = jnp.transpose(cf[lanes, rows]) * scale_g

    def take(c, carry):
        send_x(c).wait()

        @pl.when(c + DEPTH < plan.chunks)
        def _():
            send_x(c + DEPTH).start()

        @pl.when(c == plan.events[0])
        def _():
            to_z.wait()
            cp[pl.ds(keep, quarter), :] += r2[...]
            to_x.start()

        @pl.when(c == plan.events[1])
        def _():
            to_x.wait()
            cf[pl.ds(keep, quarter), :] = cp[pl.ds(keep, quarter), :] + r3[...]
            back_z.start()

        @pl.when(c == plan.events[2])
        def _():
            back_z.wait_send()
            came_z.wait_recv()
            back_core.start()
            back_core.wait_send()
            came_core.wait_recv()

            @pl.when(hi == 0)
            def _():
                each(0, EX_DEV * EX_DEV, lambda i: scaled(i))

            @pl.when(hi == 1)
            def _():
                each(0, EX_DEV * EX_DEV, lambda i: turn_scaled(i))

        for rows, count, to in ((small, plan.x_panels[1], prod_l), (large, plan.x_panels[0], prod_s)):
            begin = SURE_PANELS * (rows - BASE)

            def sure_end(k):
                return jnp.minimum(k * plan.chunk // (rows - BASE), SURE_PANELS)

            def full_end(k):
                more = jnp.maximum(k * plan.chunk - begin, 0) // rows
                return SURE_PANELS + jnp.minimum(more, count - SURE_PANELS)

            each(sure_end(c), sure_end(c + 1), functools.partial(panel_part, rows=rows, to=to, sure=True))
            if count > SURE_PANELS:
                each(full_end(c), full_end(c + 1), functools.partial(panel_part, rows=rows, to=to, sure=False))
        return carry

    lax.fori_loop(0, plan.chunks, take, 0)
    step_rows = 32 if size % 32 == 0 else 16
    scale_x = 1.0 / jnp.sqrt(jnp.full((step_rows, LEN), float(FF), F32))

    def weigh(i):
        rows = pl.ds(pl.multiple_of(i * step_rows, step_rows), step_rows)
        for b in range(EX_DEV):
            lanes = slice(b * LEN, (b + 1) * LEN)
            gram = lax.select_n(is_large, prod_s[rows, lanes], prod_l[rows, lanes])
            product = (gram * scale_x) * gg[rows, lanes]
            for a in range(EX_DEV):
                acc[a : a + 1, lanes] += jnp.sum(product * wl[a, rows, :], axis=0, keepdims=True)

    each(0, size // step_rows, weigh)
    lane = iota((8, LEN), 1)
    found, right = acc[...], right_ref[...]
    out = blk_ref[...]
    for a in range(EX_DEV):
        summed = jnp.sum(right * found[a : a + 1, :], axis=1, keepdims=True)
        out = out + jnp.where(lane == a, summed, 0.0)
        summed = jnp.sum(found * right[a : a + 1, :], axis=1, keepdims=True)
        out = out + jnp.where(lane == 4 + a, summed, 0.0)
    tile[...] = out
    mine = hi * 8 + me

    def tell(i):
        to = lax.rem(mine + i, 16)
        other = lax.rem(to, 8)
        side = to // 8
        device = (other // 4, lax.rem(e, 8) + 8 * side, lax.rem(other, 4))
        return remote(tile, gather.at[mine], t_send.at[i], t_recv.at[mine], device)

    for i in range(1, 16):
        tell(i).start()
    gather[mine] = out
    for i in range(1, 16):
        came = lax.rem(mine + i, 16)
        remote(tile, gather.at[came], t_send.at[i], t_recv.at[came], partner).wait_recv()
    whole = gather[8 * hi]
    across = gather[8 - 8 * hi]
    for i in range(1, 8):
        whole = whole + gather[8 * hi + i]
        across = across + gather[8 - 8 * hi + i]
    out_ref[:, 0:4] = whole[:4, 0:4] + across[:4, 4:8]
    out_ref[:, 4:8] = whole[:4, 8:12]
    for i in range(1, 16):
        tell(i).wait_send()
    each(0, G_CHUNKS, lambda c: send_g(c).wait_send())


def vmem():
    return pl.BlockSpec(memory_space=pltpu.VMEM)


def hbm():
    return pl.BlockSpec(memory_space=pl.ANY)


def smem():
    return pl.BlockSpec(memory_space=pltpu.SMEM)


def run_first(lengths, feats, grads):
    dma = pltpu.SemaphoreType.DMA
    return pl.pallas_call(
        first_kernel,
        name="block_part",
        out_shape=(
            jax.ShapeDtypeStruct((BASE, SURE_PANELS * PANEL), BF16),
            jax.ShapeDtypeStruct((ROWS, ROWS), BF16),
            jax.ShapeDtypeStruct((8, LEN), F32),
            jax.ShapeDtypeStruct((8, LEN), jnp.int32),
            jax.ShapeDtypeStruct((1,), jnp.int32),
        ),
        in_specs=[smem(), hbm(), hbm()],
        out_specs=(hbm(), vmem(), vmem(), vmem(), smem()),
        scratch_shapes=[
            pltpu.VMEM((F_TP, ROWS, WIDE), BF16),
            pltpu.VMEM((D_TP, ROWS, WIDE), BF16),
            pltpu.VMEM((BASE, SURE_PANELS * PANEL), BF16),
            pltpu.VMEM((LEN, 6 * LEN), F32),
            pltpu.VMEM((LEN, 6 * LEN), F32),
            pltpu.VMEM((LEN // 2, 6 * LEN), F32),
            pltpu.VMEM((LEN // 2, 6 * LEN), F32),
            pltpu.VMEM((LEN // 2, 6 * LEN), F32),
            pltpu.VMEM((8, LEN), jnp.int32),
            pltpu.VMEM((8, LEN), jnp.int32),
            pltpu.VMEM((3, 8, LEN), jnp.int32),
            pltpu.VMEM((3, 8, LEN), jnp.int32),
            dma((F_TP + D_TP,)),
            dma((1,)),
            dma((EX_DEV,)),
            dma((EX_DEV,)),
            dma((3,)),
            dma((3,)),
            dma((6,)),
            dma((6,)),
        ],
        compiler_params=pltpu.CompilerParams(collective_id=0, has_side_effects=True, vmem_limit_bytes=56 << 20),
    )(lengths, feats, grads)


def run_second(number, lengths, far_len, blk, pick, near, feats, grads):
    dma = pltpu.SemaphoreType.DMA
    plan = Plan(*VARIANTS[number])
    stream, g_stream = plan.chunk * plan.chunks, plan.g_chunk * G_CHUNKS
    tall = pltpu.VMEM((plan.large, ROWS), F32)
    square = pltpu.VMEM((ROWS, ROWS), F32)
    return pl.pallas_call(
        functools.partial(second_kernel, plan),
        name="cross_part_%d_%d" % plan.rows,
        out_shape=jax.ShapeDtypeStruct((4, 8), F32),
        in_specs=[smem()] + [hbm()] * 6,
        out_specs=vmem(),
        scratch_shapes=[
            pltpu.VMEM((X_PANELS, ROWS, PANEL), BF16),
            pltpu.VMEM((G_PANELS // 2, ROWS, 2 * NARROW), BF16),
            pltpu.VMEM((X_PANELS, ROWS, PANEL), BF16),
            pltpu.VMEM((G_PANELS, ROWS, NARROW), BF16),
            pltpu.VMEM((stream, PANEL), BF16),
            pltpu.VMEM((g_stream, NARROW), BF16),
            pltpu.VMEM((stream, PANEL), BF16),
            pltpu.VMEM((g_stream, NARROW), BF16),
            pltpu.VMEM((SURE_PANELS, BASE, PANEL), BF16),
            square,
            square,
            square,
            pltpu.VMEM((plan.grid // 2, ROWS), F32),
            pltpu.VMEM((plan.grid // 4, ROWS), F32),
            pltpu.VMEM((plan.grid // 4, ROWS), F32),
            tall,
            tall,
            tall,
            tall,
            pltpu.VMEM((EX_DEV, plan.large, LEN), F32),
            pltpu.VMEM((8, ROWS), F32),
            pltpu.VMEM((8, ROWS), F32),
            pltpu.VMEM((8, LEN), F32),
            pltpu.VMEM((16, 8, LEN), F32),
            pltpu.VMEM((ROWS, ROWS), BF16),
            pltpu.VMEM((8, LEN), jnp.int32),
            pltpu.VMEM((8, LEN), F32),
            dma((3,)),
            dma((G_PANELS,)),
            dma((X_PANELS,)),
            dma((SURE_PANELS,)),
            dma((G_CHUNKS,)),
            dma((G_CHUNKS,)),
            dma((plan.chunks,)),
            dma((plan.chunks,)),
            dma((5,)),
            dma((5,)),
            dma((16,)),
            dma((16,)),
        ],
        compiler_params=pltpu.CompilerParams(
            collective_id=number + 1, has_side_effects=True, vmem_limit_bytes=60 << 20
        ),
    )(lengths, far_len, blk, pick, near, feats, grads)


def on_device(activations, out_grads, lengths):
    feats, grads = activations[0], out_grads[0]
    near, pick, blk, far_len, which = run_first(lengths, feats, grads)
    branches = [functools.partial(run_second, number) for number in range(len(VARIANTS))]
    out = lax.switch(which[0], branches, lengths, far_len, blk, pick, near, feats, grads)
    return out[:, 4:8], out[:, 0:4]


def solution(mesh):
    placed = (P("section", "ex", "tp"), P("section", "ex", "tp"), P("ex"))
    return jax.shard_map(
        on_device,
        mesh=mesh,
        in_specs=placed,
        out_specs=(P("ex", None), P("ex", None)),
        check_vma=False,
    )
```

```python
import functools

import jax
import jax.numpy as jnp
from jax import lax
from jax.experimental import pallas as pl
from jax.experimental.pallas import tpu as pltpu
from jax.sharding import PartitionSpec as P

D = 8192
FF = 28672
LEN = 128
EX_DEV = 4
ROWS = EX_DEV * LEN
WIDE = 512
PANEL = 256
NARROW = 128
F_TP = 14
D_TP = 4
X_PANELS = 28
G_PANELS = 16
SURE = 16
BASE = EX_DEV * SURE
SURE_PANELS = 12
G_CHUNKS = 2
DEPTH = 5
TURN = 288
VARIANTS = (
    (384, 288),
    (400, 304),
    (416, 320),
    (400, 352),
    (448, 336),
    (464, 352),
    (448, 384),
    (480, 416),
    (512, 512),
)
MESH = pl.DeviceIdType.MESH
F32 = jnp.float32
BF16 = jnp.bfloat16


def dot_nt(left, right):
    return lax.dot_general(left, right, (((1,), (1,)), ((), ())), preferred_element_type=F32)


def place():
    s = lax.axis_index("section")
    e = lax.axis_index("ex")
    t = lax.axis_index("tp")
    return s, e, t


def remote(src, dst, send, recv, device):
    return pltpu.make_async_remote_copy(
        src_ref=src, dst_ref=dst, send_sem=send, recv_sem=recv, device_id=device, device_id_type=MESH
    )


def greet(peers):
    barrier = pltpu.get_barrier_semaphore()
    for peer in peers:
        pl.semaphore_signal(barrier, inc=1, device_id=peer, device_id_type=MESH)
    return lambda: pl.semaphore_wait(barrier, len(peers))


def iota(shape, dim):
    return lax.broadcasted_iota(jnp.int32, shape, dim)


def block_tiles(rows_ref, j, out_ref):
    at = 0
    for a in range(EX_DEV - 1):
        width = (EX_DEV - 1 - a) * LEN
        out_ref[:, at : at + width] += dot_nt(
            rows_ref[j, a * LEN : (a + 1) * LEN, :], rows_ref[j, (a + 1) * LEN :, :]
        )
        at += width


def first_kernel(
    lens, x_hbm, g_hbm,
    near_hbm, pick_ref, blk_ref, far_len_ref, which_ref,
    xraw, graw, near, xd, gd, r_core, r_z, r_back, lt, mt, lx, ly,
    ld_sem, out_sem, s_send, s_recv, d_send, d_recv, l_send, l_recv,
):
    s, e, t = place()
    x, y = e // 4, lax.rem(e, 4)
    hi = e // 8
    core, z = lax.rem(t, 2), t // 2
    partner = (s, lax.rem(e + 8, 16), t)
    core_peer = (s, e, t + 1 - 2 * core)
    z_peer = (s, e, lax.rem(t + 2, 4))
    x_peers = [(s, lax.rem(x + d, 4) * 4 + y, t) for d in (1, 2, 3)]
    y_peers = [(s, x * 4 + lax.rem(y + d, 4), t) for d in (1, 2, 3)]
    met = greet(x_peers + y_peers + [core_peer, z_peer])

    def load(ref, to, j, at):
        return pltpu.make_async_copy(ref.at[:, pl.ds(pl.multiple_of(j * WIDE, WIDE), WIDE)], to.at[j], ld_sem.at[at + j])

    for j in range(D_TP):
        load(g_hbm, graw, j, 0).start()
    for j in range(F_TP):
        load(x_hbm, xraw, j, D_TP).start()

    counts = [lens[j] for j in range(EX_DEV)]
    starts = [jnp.int32(BASE)]
    for j in range(EX_DEV):
        starts.append(starts[-1] + counts[j] - SURE)
    row = iota((8, LEN), 0)
    mine = jnp.full((8, LEN), starts[EX_DEV], jnp.int32)
    for j in range(EX_DEV):
        mine = jnp.where(row == j, counts[j], mine)
    lt[...] = mine
    xd[...] = jnp.zeros_like(xd)
    gd[...] = jnp.zeros_like(gd)

    def gram_g(j, carry):
        load(g_hbm, graw, j, 0).wait()
        block_tiles(graw, j, gd)
        return carry

    lax.fori_loop(0, D_TP, gram_g, 0)
    met()
    for i, peer in enumerate(x_peers):
        remote(lt, lx.at[i], l_send.at[i], l_recv.at[i], peer).start()

    def send_x(j):
        rows = pl.ds(j * SURE, SURE)
        at = pl.multiple_of(hi * (X_PANELS - SURE_PANELS) * PANEL, PANEL)
        source = x_hbm.at[pl.ds(j * LEN, SURE), pl.ds(at, SURE_PANELS * PANEL)]
        return remote(source, near.at[rows], s_send.at[j], s_recv.at[j], partner)

    for j in range(EX_DEV):
        send_x(j).start()
    half = LEN // 2
    keep = pl.multiple_of(core * half, half)
    give = pl.multiple_of((1 - core) * half, half)
    to_core = remote(gd.at[pl.ds(give, half)], r_core, d_send.at[0], d_recv.at[0], core_peer)
    to_core.start()
    for b in range(EX_DEV):
        packed = iota((LEN, LEN), 0) + b * LEN
        source = jnp.full((LEN, LEN), -1, jnp.int32)
        for j in reversed(range(EX_DEV)):
            source = jnp.where(packed < starts[j + 1], packed - starts[j] + j * LEN + SURE, source)
        if b * LEN < BASE:
            source = jnp.where(packed < BASE, packed // SURE * LEN + lax.rem(packed, SURE), source)
        for c in range(EX_DEV):
            pick_ref[b * LEN : (b + 1) * LEN, c * LEN : (c + 1) * LEN] = jnp.where(
                source == iota((LEN, LEN), 1) + c * LEN, 1.0, 0.0
            ).astype(BF16)
    to_core.wait()
    gd[pl.ds(keep, half), :] += r_core[...]
    for i in range(3):
        remote(lt, lx.at[i], l_send.at[i], l_recv.at[i], x_peers[i]).wait_recv()
    smaller = jnp.maximum(jnp.minimum(lt[...], lx[1]), jnp.minimum(lx[0], lx[2]))
    larger = jnp.maximum(jnp.maximum(lt[...], lx[0]), jnp.maximum(lx[1], lx[2]))
    mt[...] = jnp.where(row == 5, smaller, larger)
    far_len_ref[...] = lx[1]
    to_z = remote(gd.at[pl.ds(keep, half)], r_z, d_send.at[1], d_recv.at[1], z_peer)
    to_z.start()
    for i, peer in enumerate(y_peers):
        remote(mt, ly.at[i], l_send.at[3 + i], l_recv.at[3 + i], peer).start()

    def gram_x(j, carry):
        load(x_hbm, xraw, j, D_TP).wait()
        block_tiles(xraw, j, xd)
        return carry

    lax.fori_loop(0, F_TP, gram_x, 0)
    swap = remote(xd.at[pl.ds(give, half)], r_back, d_send.at[2], d_recv.at[2], core_peer)
    swap.start()
    to_z.wait()
    gd[pl.ds(keep, half), :] += r_z[...]
    for i in range(3):
        remote(mt, ly.at[i], l_send.at[3 + i], l_recv.at[3 + i], y_peers[i]).wait_recv()
    most = jnp.maximum(jnp.maximum(mt[...], ly[0]), jnp.maximum(ly[1], ly[2]))
    which = jnp.full((1, LEN), len(VARIANTS) - 1, jnp.int32)
    for i in reversed(range(len(VARIANTS) - 1)):
        fits = (most[4:5, :] <= VARIANTS[i][0]) & (most[5:6, :] <= VARIANTS[i][1])
        which = jnp.where(fits, i, which)
    which_ref[0] = jnp.max(which)
    swap.wait()
    xd[pl.ds(keep, half), :] += r_back[...]
    blk = jnp.zeros((8, LEN), F32)
    lane = iota((8, LEN), 1)
    inner_row = iota((half, LEN), 0) + keep
    inner_lane = iota((half, LEN), 1)
    scale_x = 1.0 / jnp.sqrt(jnp.full((half, LEN), float(FF), F32))
    scale_g = 1.0 / jnp.sqrt(jnp.full((half, LEN), float(D), F32))
    inverse = [1.0 / jnp.sqrt(jnp.full((8, LEN), counts[j].astype(F32), F32)) for j in range(EX_DEV)]
    at = 0
    for a in range(EX_DEV - 1):
        for b in range(a + 1, EX_DEV):
            rows, lanes = pl.ds(keep, half), slice(at, at + LEN)
            product = (xd[rows, lanes] * scale_x) * (gd[rows, lanes] * scale_g)
            live = (inner_row < counts[a]) & (inner_lane < counts[b])
            product = jnp.where(live, product, 0.0)
            total = jnp.sum(jnp.sum(product, axis=0, keepdims=True), axis=1, keepdims=True)
            spot = ((row == a) & (lane == 8 + b)) | ((row == b) & (lane == 8 + a))
            blk = blk + jnp.where(spot, jnp.broadcast_to(total, (8, LEN)) * inverse[a] * inverse[b], 0.0)
            at += LEN
    blk_ref[...] = blk
    for j in range(EX_DEV):
        send_x(j).wait()
    out = pltpu.make_async_copy(near, near_hbm, out_sem.at[0])
    out.start()
    for i in range(3):
        remote(lt, lx.at[i], l_send.at[i], l_recv.at[i], x_peers[i]).wait_send()
        remote(mt, ly.at[i], l_send.at[3 + i], l_recv.at[3 + i], y_peers[i]).wait_send()
    out.wait()


def up(value, step):
    return -(-value // step) * step


class Plan:
    def __init__(self, large, small):
        self.large, self.small = large, small
        self.grid = up(large, 32)
        self.lanes = up(small, 128)
        c = min(range(SURE_PANELS, X_PANELS // 2 + 1), key=lambda c: max(c * large, (X_PANELS - c) * small))
        d = min(range(1, G_PANELS // 2 + 1), key=lambda d: max(d * large, (G_PANELS - d) * small))
        self.g_panels = (d, G_PANELS - d)
        self.x_panels = (c, X_PANELS - c)
        self.rows = (large, small)
        ends = [self.offset(r, n) for r, n in zip(self.rows, self.x_panels)]
        units = up(max(ends), 16) // 16
        self.chunks = min(range(11, 18), key=lambda n: (up(units, n), -n))
        self.chunk = up(units, self.chunks) // self.chunks * 16
        self.events = (1, self.chunks * 6 // 14, self.chunks * 9 // 14)
        g_ends = [r * n for r, n in zip(self.rows, self.g_panels)]
        self.g_chunk = up(max(g_ends) // 16, G_CHUNKS) // G_CHUNKS * 16

    def offset(self, rows, panel):
        return panel * rows - BASE * min(panel, SURE_PANELS)


def pieces(total, bounds_a, bounds_b):
    cuts = sorted({0, total} | {b for b in bounds_a + bounds_b if b < total})
    return list(zip(cuts, cuts[1:]))


def spot(bounds, first, at):
    panel = 0
    while panel + 1 < len(bounds) and bounds[panel + 1] <= at:
        panel += 1
    return panel, first[panel] + at - bounds[panel]


def second_kernel(
    plan, lens, far_len_hbm, blk_hbm, pick_hbm, near_hbm, x_hbm, g_hbm,
    out_ref,
    xraw, graw, xp, gp, sx, sg, fx, fg, nr, cp, cf, gg, r1, r2, r3, prod_l, prod_s, gram_l, gram_s,
    wl, acc, right_ref, tile, gather, pick, far_len, blk_ref,
    in_sem, ld_sem, lx_sem, near_sem, g_send, g_recv, x_send, x_recv, r_send, r_recv, t_send, t_recv,
):
    large, small = plan.rows
    size = large
    s, e, t = place()
    hi = e // 8
    core, z = lax.rem(t, 2), t // 2
    partner = (s, lax.rem(e + 8, 16), t)
    core_peer = (s, e, t + 1 - 2 * core)
    z_peer = (s, e, lax.rem(t + 2, 4))
    me = s * 4 + t
    column = []
    for d in range(1, 8):
        other = lax.rem(me + d, 8)
        column.append((other // 4, e, lax.rem(other, 4)))
    met = greet([partner] + column)

    def load_g(j):
        at = pl.multiple_of(jnp.where(hi == 0, j, G_PANELS - 1 - j) * NARROW, NARROW)
        to = graw.at[j // 2, :, pl.ds(pl.multiple_of(lax.rem(j, 2) * NARROW, NARROW), NARROW)]
        return pltpu.make_async_copy(g_hbm.at[:, pl.ds(at, NARROW)], to, ld_sem.at[j])

    def load_x(j):
        at = pl.multiple_of(jnp.where(hi == 0, j, X_PANELS - 1 - j) * PANEL, PANEL)
        return pltpu.make_async_copy(x_hbm.at[:, pl.ds(at, PANEL)], xraw.at[j], lx_sem.at[j])

    def load_near(j):
        at = pl.multiple_of(jnp.where(hi == 0, SURE_PANELS - 1 - j, j) * PANEL, PANEL)
        return pltpu.make_async_copy(near_hbm.at[:, pl.ds(at, PANEL)], nr.at[j], near_sem.at[j])

    def each(first, last, fn):
        def body(j, carry):
            fn(j)
            return carry

        lax.fori_loop(first, last, body, 0)

    loads = [
        pltpu.make_async_copy(pick_hbm, pick, in_sem.at[0]),
        pltpu.make_async_copy(far_len_hbm, far_len, in_sem.at[1]),
        pltpu.make_async_copy(blk_hbm, blk_ref, in_sem.at[2]),
    ]
    for copy in loads:
        copy.start()
    each(0, G_PANELS, lambda j: load_g(j).start())
    each(0, X_PANELS, lambda j: load_x(j).start())
    each(0, SURE_PANELS, lambda j: load_near(j).start())

    def packed(raw, put):
        top = min(size, TURN)
        put(slice(0, top), jnp.dot(pick[0:top, :], raw[...], preferred_element_type=F32).astype(BF16))
        rest = jnp.dot(pick[top:size, ROWS // 2 :], raw[ROWS // 2 :, :], preferred_element_type=F32)
        put(slice(top, size), rest.astype(BF16))

    def pack_g(c):
        load_g(2 * c).wait()
        load_g(2 * c + 1).wait()

        def put(rows, value):
            gp[2 * c, rows, :] = value[:, :NARROW]
            gp[2 * c + 1, rows, :] = value[:, NARROW:]

        packed(graw.at[c], put)

    def pack_x(c):
        load_x(c).wait()

        def put(rows, value):
            xp[c, rows, :] = value

        packed(xraw.at[c], put)

    for copy in loads:
        copy.wait()
    own_total = lens[0] + lens[1] + lens[2] + lens[3]
    far_total = jnp.max(far_len[...])
    is_large = (own_total > far_total) | ((own_total == far_total) & (hi == 0))

    def fill(to, source, chunk, count, bounds, first):
        for a, b in pieces(chunk * count, *bounds):
            (pa, ra), (pb, rb) = spot(bounds[0], first[0], a), spot(bounds[1], first[1], a)
            if ra + b - a > large:
                pa, ra = pb, rb
            if rb + b - a > large:
                pb, rb = pa, ra
            if ra + b - a > large:
                pa, ra, pb, rb = 0, 0, 0, 0
            to[a:b, :] = lax.select_n(is_large, source[pb, rb : rb + b - a, :], source[pa, ra : ra + b - a, :])

    def send_g(c):
        rows = pl.ds(pl.multiple_of(c * plan.g_chunk, 16), plan.g_chunk)
        return remote(sg.at[rows], fg.at[rows], g_send.at[c], g_recv.at[c], partner)

    def send_x(c):
        rows = pl.ds(pl.multiple_of(c * plan.chunk, 16), plan.chunk)
        return remote(sx.at[rows], fx.at[rows], x_send.at[c], x_recv.at[c], partner)

    g_bounds = [[p * r for p in range(n + 1)] for r, n in zip(plan.rows, plan.g_panels)]
    x_bounds = [[plan.offset(r, p) for p in range(n + 1)] for r, n in zip(plan.rows, plan.x_panels)]
    x_first = [[BASE if p < SURE_PANELS else 0 for p in range(len(b))] for b in x_bounds]
    first_g = up(plan.g_panels[1], 2) // 2
    each(0, first_g, pack_g)
    fill(sg, gp, plan.g_chunk, G_CHUNKS, g_bounds, [[0] * len(b) for b in g_bounds])
    met()
    each(0, G_CHUNKS, lambda k: send_g(k).start())
    each(first_g, G_PANELS // 2, pack_g)

    def all_x(c):
        pack_x(c)

        @pl.when(c == plan.x_panels[1] - 1)
        def _():
            fill(sx, xp, plan.chunk, plan.chunks, x_bounds, x_first)
            each(0, DEPTH, lambda k: send_x(k).start())

    each(0, X_PANELS, all_x)
    if size < ROWS:

        def clear_g(p):
            gp[p, size:, :] = jnp.zeros((ROWS - size, NARROW), BF16)

        def clear_x(p):
            xp[p, size:, :] = jnp.zeros((ROWS - size, PANEL), BF16)

        each(0, G_PANELS, clear_g)
        each(0, X_PANELS, clear_x)
        if plan.grid < ROWS:
            cf[plan.grid :, :] = jnp.zeros((ROWS - plan.grid, ROWS), F32)
    if plan.lanes < ROWS:
        cf[:, plan.lanes :] = jnp.zeros((ROWS, ROWS - plan.lanes), F32)
    acc[...] = jnp.zeros_like(acc)
    wide_row, wide_lane = iota((8, ROWS), 0), iota((8, ROWS), 1)
    right = jnp.zeros((8, ROWS), F32)
    begin = jnp.int32(BASE)
    for b in range(EX_DEV):
        count = lens[b]
        inverse = 1.0 / jnp.sqrt(jnp.full((8, ROWS), count.astype(F32), F32))
        end = begin + count - SURE
        sure = (wide_lane >= b * SURE) & (wide_lane < (b + 1) * SURE)
        inside = (wide_row == b) & (sure | ((wide_lane >= begin) & (wide_lane < end)))
        right = jnp.where(inside, inverse, right)
        begin = end
    right_ref[...] = right
    each(0, SURE_PANELS, lambda j: load_near(j).wait())
    def clear(i):
        rows = pl.ds(pl.multiple_of(i * 16, 16), 16)
        for ref in (prod_s, prod_l):
            ref[rows, :] = jnp.zeros((16, ROWS), F32)

    def clear_square(i):
        rows = pl.ds(pl.multiple_of(i * 16, 16), 16)
        for ref in (gram_s, gram_l):
            ref[rows, :] = jnp.zeros((16, ROWS), F32)

    each(0, size // 16, clear)
    each(0, ROWS // 16, clear_square)

    def near_part(p):
        prod_s[0:BASE, :] += dot_nt(nr[p], xp[X_PANELS - 1 - p])

    each(0, SURE_PANELS, near_part)
    prod_l[0:BASE, :] = prod_s[0:BASE, :]
    begin = jnp.full((1, LEN), BASE, jnp.int32)
    for a in range(EX_DEV):
        count = far_len[a : a + 1, :]
        inverse = 1.0 / jnp.sqrt(count.astype(F32))
        rows = iota((size, LEN), 0)
        end = begin + count - SURE
        sure = (rows >= a * SURE) & (rows < (a + 1) * SURE)
        wl[a] = jnp.where(sure | ((rows >= begin) & (rows < end)), inverse, 0.0)
        begin = end
    each(0, G_CHUNKS, lambda c: send_g(c).wait_recv())
    half, quarter = plan.grid // 2, plan.grid // 4
    for rows, count, to in ((small, plan.g_panels[1], gram_l), (large, plan.g_panels[0], gram_s)):

        def gram_part(p, rows=rows, to=to):
            at = pl.multiple_of(p * rows, 16)
            to[0:rows, :] += dot_nt(fg[pl.ds(at, rows), :], gp[G_PANELS - 1 - p])

        each(0, count, gram_part)

    def spans(i):
        i, j = i // EX_DEV, lax.rem(i, EX_DEV)
        return pl.ds(pl.multiple_of(i * LEN, LEN), LEN), pl.ds(pl.multiple_of(j * LEN, LEN), LEN)

    def by_role(i):
        rows, lanes = spans(i)
        cp[rows, lanes] = lax.select_n(is_large, gram_s[rows, lanes], jnp.transpose(gram_l[lanes, rows]))

    each(0, EX_DEV * EX_DEV, by_role)
    live = pl.ds(0, plan.lanes)
    keep_half = pl.multiple_of(core * half, 8)
    give_half = pl.multiple_of((1 - core) * half, 8)
    keep = pl.multiple_of(core * half + z * quarter, 8)
    give = pl.multiple_of(core * half + (1 - z) * quarter, 8)

    step = remote(cp.at[pl.ds(give_half, half), live], r1, r_send.at[0], r_recv.at[0], core_peer)
    step.start()
    step.wait()
    cp[pl.ds(keep_half, half), live] += r1[...]
    to_z = remote(cp.at[pl.ds(give, quarter), live], r2, r_send.at[1], r_recv.at[1], z_peer)
    to_z.start()

    to_x = remote(cp.at[pl.ds(keep, quarter), live], r3, r_send.at[2], r_recv.at[2], partner)
    back_z = remote(cf.at[pl.ds(keep, quarter), live], cf.at[pl.ds(keep, quarter), live], r_send.at[3], r_recv.at[3], z_peer)
    came_z = remote(cf.at[pl.ds(keep, quarter), live], cf.at[pl.ds(give, quarter), live], r_send.at[3], r_recv.at[3], z_peer)
    back_core = remote(
        cf.at[pl.ds(keep_half, half), live], cf.at[pl.ds(keep_half, half), live], r_send.at[4], r_recv.at[4], core_peer
    )
    came_core = remote(
        cf.at[pl.ds(keep_half, half), live], cf.at[pl.ds(give_half, half), live], r_send.at[4], r_recv.at[4], core_peer
    )

    def panel_part(p, rows, to, sure):
        first = BASE if sure else 0
        at = p * rows - BASE * (p if sure else SURE_PANELS)
        far = fx[pl.ds(pl.multiple_of(at, 16), rows - first), :]
        to[first:rows, :] += dot_nt(far, xp[X_PANELS - 1 - p])

    scale_g = 1.0 / jnp.sqrt(jnp.full((LEN, LEN), float(D), F32))

    def scaled(i):
        rows, lanes = spans(i)
        gram = lax.select_n(is_large, cf[rows, lanes], jnp.transpose(cf[lanes, rows]))
        gg[rows, lanes] = gram * scale_g

    def take(c, carry):
        send_x(c).wait()

        @pl.when(c + DEPTH < plan.chunks)
        def _():
            send_x(c + DEPTH).start()

        @pl.when(c == plan.events[0])
        def _():
            to_z.wait()
            cp[pl.ds(keep, quarter), live] += r2[...]
            to_x.start()

        @pl.when(c == plan.events[1])
        def _():
            to_x.wait()
            cf[pl.ds(keep, quarter), live] = cp[pl.ds(keep, quarter), live] + r3[...]
            back_z.start()

        @pl.when(c == plan.events[2])
        def _():
            back_z.wait_send()
            came_z.wait_recv()
            back_core.start()
            back_core.wait_send()
            came_core.wait_recv()

            each(0, EX_DEV * EX_DEV, scaled)

        for rows, count, to in ((small, plan.x_panels[1], prod_l), (large, plan.x_panels[0], prod_s)):
            begin = SURE_PANELS * (rows - BASE)

            def sure_end(k):
                return jnp.minimum(k * plan.chunk // (rows - BASE), SURE_PANELS)

            def full_end(k):
                more = jnp.maximum(k * plan.chunk - begin, 0) // rows
                return SURE_PANELS + jnp.minimum(more, count - SURE_PANELS)

            each(sure_end(c), sure_end(c + 1), functools.partial(panel_part, rows=rows, to=to, sure=True))
            if count > SURE_PANELS:
                each(full_end(c), full_end(c + 1), functools.partial(panel_part, rows=rows, to=to, sure=False))
        return carry

    lax.fori_loop(0, plan.chunks, take, 0)
    step_rows = 32 if size % 32 == 0 else 16
    scale_x = 1.0 / jnp.sqrt(jnp.full((step_rows, LEN), float(FF), F32))

    def weigh(i):
        rows = pl.ds(pl.multiple_of(i * step_rows, step_rows), step_rows)
        for b in range(EX_DEV):
            lanes = slice(b * LEN, (b + 1) * LEN)
            gram = lax.select_n(is_large, prod_s[rows, lanes], prod_l[rows, lanes])
            product = (gram * scale_x) * gg[rows, lanes]
            for a in range(EX_DEV):
                acc[a : a + 1, lanes] += jnp.sum(product * wl[a, rows, :], axis=0, keepdims=True)

    each(0, size // step_rows, weigh)
    lane = iota((8, LEN), 1)
    found, right = acc[...], right_ref[...]
    out = blk_ref[...]
    for a in range(EX_DEV):
        summed = jnp.sum(right * found[a : a + 1, :], axis=1, keepdims=True)
        out = out + jnp.where(lane == a, summed, 0.0)
        summed = jnp.sum(found * right[a : a + 1, :], axis=1, keepdims=True)
        out = out + jnp.where(lane == 4 + a, summed, 0.0)
    tile[...] = out
    mine = hi * 8 + me

    def tell(i):
        to = lax.rem(mine + i, 16)
        other = lax.rem(to, 8)
        side = to // 8
        device = (other // 4, lax.rem(e, 8) + 8 * side, lax.rem(other, 4))
        return remote(tile, gather.at[mine], t_send.at[i], t_recv.at[mine], device)

    for i in range(1, 16):
        tell(i).start()
    gather[mine] = out
    for i in range(1, 16):
        came = lax.rem(mine + i, 16)
        remote(tile, gather.at[came], t_send.at[i], t_recv.at[came], partner).wait_recv()
    whole = gather[8 * hi]
    across = gather[8 - 8 * hi]
    for i in range(1, 8):
        whole = whole + gather[8 * hi + i]
        across = across + gather[8 - 8 * hi + i]
    out_ref[:, 0:4] = whole[:4, 0:4] + across[:4, 4:8]
    out_ref[:, 4:8] = whole[:4, 8:12]
    for i in range(1, 16):
        tell(i).wait_send()
    each(0, G_CHUNKS, lambda c: send_g(c).wait_send())


def vmem():
    return pl.BlockSpec(memory_space=pltpu.VMEM)


def hbm():
    return pl.BlockSpec(memory_space=pl.ANY)


def smem():
    return pl.BlockSpec(memory_space=pltpu.SMEM)


def run_first(lengths, feats, grads):
    dma = pltpu.SemaphoreType.DMA
    return pl.pallas_call(
        first_kernel,
        name="block_part",
        out_shape=(
            jax.ShapeDtypeStruct((BASE, SURE_PANELS * PANEL), BF16),
            jax.ShapeDtypeStruct((ROWS, ROWS), BF16),
            jax.ShapeDtypeStruct((8, LEN), F32),
            jax.ShapeDtypeStruct((8, LEN), jnp.int32),
            jax.ShapeDtypeStruct((1,), jnp.int32),
        ),
        in_specs=[smem(), hbm(), hbm()],
        out_specs=(hbm(), vmem(), vmem(), vmem(), smem()),
        scratch_shapes=[
            pltpu.VMEM((F_TP, ROWS, WIDE), BF16),
            pltpu.VMEM((D_TP, ROWS, WIDE), BF16),
            pltpu.VMEM((BASE, SURE_PANELS * PANEL), BF16),
            pltpu.VMEM((LEN, 6 * LEN), F32),
            pltpu.VMEM((LEN, 6 * LEN), F32),
            pltpu.VMEM((LEN // 2, 6 * LEN), F32),
            pltpu.VMEM((LEN // 2, 6 * LEN), F32),
            pltpu.VMEM((LEN // 2, 6 * LEN), F32),
            pltpu.VMEM((8, LEN), jnp.int32),
            pltpu.VMEM((8, LEN), jnp.int32),
            pltpu.VMEM((3, 8, LEN), jnp.int32),
            pltpu.VMEM((3, 8, LEN), jnp.int32),
            dma((F_TP + D_TP,)),
            dma((1,)),
            dma((EX_DEV,)),
            dma((EX_DEV,)),
            dma((3,)),
            dma((3,)),
            dma((6,)),
            dma((6,)),
        ],
        compiler_params=pltpu.CompilerParams(collective_id=0, has_side_effects=True, vmem_limit_bytes=56 << 20),
    )(lengths, feats, grads)


def run_second(number, lengths, far_len, blk, pick, near, feats, grads):
    dma = pltpu.SemaphoreType.DMA
    plan = Plan(*VARIANTS[number])
    stream, g_stream = plan.chunk * plan.chunks, plan.g_chunk * G_CHUNKS
    tall = pltpu.VMEM((plan.large, ROWS), F32)
    square = pltpu.VMEM((ROWS, ROWS), F32)
    return pl.pallas_call(
        functools.partial(second_kernel, plan),
        name="cross_part_%d_%d" % plan.rows,
        out_shape=jax.ShapeDtypeStruct((4, 8), F32),
        in_specs=[smem()] + [hbm()] * 6,
        out_specs=vmem(),
        scratch_shapes=[
            pltpu.VMEM((X_PANELS, ROWS, PANEL), BF16),
            pltpu.VMEM((G_PANELS // 2, ROWS, 2 * NARROW), BF16),
            pltpu.VMEM((X_PANELS, ROWS, PANEL), BF16),
            pltpu.VMEM((G_PANELS, ROWS, NARROW), BF16),
            pltpu.VMEM((stream, PANEL), BF16),
            pltpu.VMEM((g_stream, NARROW), BF16),
            pltpu.VMEM((stream, PANEL), BF16),
            pltpu.VMEM((g_stream, NARROW), BF16),
            pltpu.VMEM((SURE_PANELS, BASE, PANEL), BF16),
            square,
            square,
            square,
            pltpu.VMEM((plan.grid // 2, plan.lanes), F32),
            pltpu.VMEM((plan.grid // 4, plan.lanes), F32),
            pltpu.VMEM((plan.grid // 4, plan.lanes), F32),
            tall,
            tall,
            square,
            square,
            pltpu.VMEM((EX_DEV, plan.large, LEN), F32),
            pltpu.VMEM((8, ROWS), F32),
            pltpu.VMEM((8, ROWS), F32),
            pltpu.VMEM((8, LEN), F32),
            pltpu.VMEM((16, 8, LEN), F32),
            pltpu.VMEM((ROWS, ROWS), BF16),
            pltpu.VMEM((8, LEN), jnp.int32),
            pltpu.VMEM((8, LEN), F32),
            dma((3,)),
            dma((G_PANELS,)),
            dma((X_PANELS,)),
            dma((SURE_PANELS,)),
            dma((G_CHUNKS,)),
            dma((G_CHUNKS,)),
            dma((plan.chunks,)),
            dma((plan.chunks,)),
            dma((5,)),
            dma((5,)),
            dma((16,)),
            dma((16,)),
        ],
        compiler_params=pltpu.CompilerParams(
            collective_id=number + 1, has_side_effects=True, vmem_limit_bytes=60 << 20
        ),
    )(lengths, far_len, blk, pick, near, feats, grads)


def on_device(activations, out_grads, lengths):
    feats, grads = activations[0], out_grads[0]
    near, pick, blk, far_len, which = run_first(lengths, feats, grads)
    branches = [functools.partial(run_second, number) for number in range(len(VARIANTS))]
    out = lax.switch(which[0], branches, lengths, far_len, blk, pick, near, feats, grads)
    return out[:, 4:8], out[:, 0:4]


def solution(mesh):
    placed = (P("section", "ex", "tp"), P("section", "ex", "tp"), P("ex"))
    return jax.shard_map(
        on_device,
        mesh=mesh,
        in_specs=placed,
        out_specs=(P("ex", None), P("ex", None)),
        check_vma=False,
    )
```
